512 devices in a mesh: dp: 64 (over y, z_lo, core), space: 8 (over x, z_hi).
Axes of the slice: x: 4, y: 4, z: 16 (z_hi: 2, z_lo: 8; z = z_hi * 8 + z_lo), core: 2. Of those that a mesh axis runs over, the one named last changes fastest.
Arguments:
- volume: float32 [64, 32, 32, 256], P('dp', None, 'space'), may hold values from -6 to 6
- cotangent: float32 [64, 64, 128], P('dp', 'space'), may hold values from -6 to 6
- w_first: float32 [64, 2048], replicated, may hold values from -0.125 to 0.125
- b_first: float32 [64], replicated, may hold values from -3 to 3
- w_second: float32 [64, 4096], P('space'), may hold values from -0.09375 to 0.09375
- b_second: float32 [64], P('space'), may hold values from -3 to 3
Outputs:
- output: float32 [64, 64, 128], P('dp', 'space')
- grad_volume: float32 [64, 32, 32, 256], P('dp', None, 'space')
- grad_w_first: float32 [64, 2048], replicated
- grad_b_first: float32 [64], replicated
- grad_w_second: float32 [64, 4096], P('space')
- grad_b_second: float32 [64], P('space')
The draws below stay inside these ranges and needn't reach their ends.
All inputs are finite; a program needn't handle non-finite values.
Results may differ from the reference program's by a relative error of at most 0.00018.
Values sent between devices are 32-bit elements; how exact they have to be, the bound alone decides.
A program may use at most 128 MiB of HBM per device.

```python
import jax
import jax.numpy as jnp
from jax import lax

CIN = 32
C1 = 64
C2 = 64
HEIGHT = 16
WIDTH = 16
SAMPLES = 64
DEPTH = 32


def shard_levels(stream_key, extent, shards, low, top_value):
    gain, own = 1.0, jax.random.fold_in(stream_key, 6)
    for dim, blocks in shards:
        heights = jnp.exp(jax.random.uniform(jax.random.fold_in(own, dim), (blocks,), jnp.float32, low / len(shards), top_value / len(shards)))
        gain = gain * jnp.repeat(heights, extent[dim] // blocks).reshape([-1 if axis == dim else 1 for axis in range(len(extent))])
    return gain


def bell_draw(stream_key, extent, spread, most, split=(), kind=jnp.bfloat16):
    drawn = spread * jax.random.normal(stream_key, extent, jnp.float32)
    if split:
        drawn = drawn * shard_levels(stream_key, extent, split, -0.22, 0.18)
    return jnp.clip(drawn, -most, most).astype(kind)


def setup_inputs(seed: int = 0) -> dict:
    keys = jax.random.split(jax.random.key(seed), 7)
    volume = bell_draw(keys[0], (SAMPLES, CIN, DEPTH, HEIGHT * WIDTH), 1.0, 6.0, ((0, 64), (2, 8)), jnp.float32)
    cotangent = bell_draw(keys[1], (SAMPLES, C2, (DEPTH // 4) * (HEIGHT // 4) * (WIDTH // 4)), 0.5, 6.0, ((0, 64), (1, 8)), jnp.float32)
    w_first = bell_draw(keys[2], (C1, CIN * 64), (CIN * 64) ** -0.5, 0.125, (), jnp.float32)
    b_first = bell_draw(keys[3], (C1,), 0.5, 3.0, (), jnp.float32)
    w_second = bell_draw(keys[4], (C2, C1 * 64), (C1 * 64) ** -0.5, 0.09375, ((0, 8),), jnp.float32)
    b_second = bell_draw(keys[5], (C2,), 0.5, 3.0, ((0, 8),), jnp.float32)
    return dict(volume=volume, cotangent=cotangent, w_first=w_first, b_first=b_first, w_second=w_second, b_second=b_second)


SLOPE = 0.3

def activate(pre_value):
    return SLOPE * pre_value + (1.0 - SLOPE) * jax.nn.softplus(pre_value)

def convolve(field, weight, bias_vector):
    out_count = weight.shape[0]
    kernel = weight.reshape(out_count, field.shape[1], 4, 4, 4)
    result = lax.conv_general_dilated(field, kernel, (2, 2, 2), [(1, 1), (1, 1), (1, 1)], dimension_numbers=('NCDHW', 'OIDHW', 'NCDHW'), precision=lax.Precision.HIGHEST)
    return result + bias_vector[None, :, None, None, None]

def reference(volume, cotangent, w_first, b_first, w_second, b_second):
    sample_count = volume.shape[0]
    volume_grid = volume.reshape(sample_count, CIN, DEPTH, HEIGHT, WIDTH)

    def forward(volume_grid, w_first, b_first, w_second, b_second):
        hidden = activate(convolve(volume_grid, w_first, b_first))
        return activate(convolve(hidden, w_second, b_second)).reshape(sample_count, C2, -1)
    output, pullback = jax.vjp(forward, volume_grid, w_first, b_first, w_second, b_second)
    grad_grid, grad_wone, grad_bone, grad_wtwo, grad_btwo = pullback(cotangent)
    sample_scale = 1.0 / SAMPLES
    return (output, grad_grid.reshape(volume.shape), grad_wone * sample_scale, grad_bone * sample_scale, grad_wtwo * sample_scale, grad_btwo * sample_scale)
```

```python
import functools

import jax
import jax.numpy as jnp
from jax import lax
from jax.experimental import pallas as pl
from jax.experimental.pallas import tpu as pltpu
from jax.sharding import PartitionSpec as P

MESH = pl.DeviceIdType.MESH
F32 = jnp.float32
BF16 = jnp.bfloat16
SLOPE = 0.3
CIN = 32
MID = 64
OWN = 8
SAMPLES = 64


def split(value):
    high = value.astype(BF16)
    low = (value - high.astype(F32)).astype(BF16)
    return high, low


def dot(a, b, contract):
    return lax.dot_general(a, b, ((contract[:1], contract[1:]), ((), ())), preferred_element_type=F32)


def smooth(pre):
    decay = jnp.exp(-jnp.abs(pre))
    soft = jnp.maximum(pre, 0.0) + jnp.log(1.0 + decay)
    return SLOPE * pre + (1.0 - SLOPE) * soft


def slope(pre):
    decay = jnp.exp(-jnp.abs(pre))
    return SLOPE + (1.0 - SLOPE) * (jnp.where(pre >= 0.0, 1.0, decay) / (1.0 + decay))


def source_of(column, tap, log_half):
    half = 1 << log_half
    width = 2 * half
    slab = lax.shift_right_logical(column, 2 * log_half)
    row = lax.shift_right_logical(column, log_half) & (half - 1)
    cell = column & (half - 1)
    high = 2 * row + lax.shift_right_logical(tap, 2) - 1
    low = 2 * cell + (tap & 3) - 1
    inside = (high >= 0) & (high < width) & (low >= 0) & (low < width)
    return jnp.where(inside, slab * (width * width) + high * width + low, -1)


def fill_pick(pick, log_half):
    @pl.loop(0, 8)
    def _(pair):
        lane = lax.broadcasted_iota(jnp.int32, (8, 256), 1)
        source = source_of(lane & 127, 2 * pair + lax.shift_right_logical(lane, 7), log_half)
        cell = lax.broadcasted_iota(jnp.int32, (512, 256), 0)
        pick[pair] = jnp.where(cell == source[0:1], 1.0, 0.0).astype(BF16)


def fill_spread(spread, log_half):
    @pl.loop(0, 8)
    def _(pair):
        row = lax.broadcasted_iota(jnp.int32, (256, 128), 0)
        source = source_of(row & 127, 2 * pair + lax.shift_right_logical(row, 7), log_half)
        cell = lax.broadcasted_iota(jnp.int32, (256, 128), 1)
        for part in range(4):
            spread[pair, :, part * 128 : (part + 1) * 128] = jnp.where(
                cell + part * 128 == source, 1.0, 0.0
            ).astype(BF16)


def columns(rows, pick, grid, channels):
    half = 4 * channels

    @pl.loop(0, 8)
    def _(pair):
        both = dot(rows[...], pick[pair], (1, 0))
        value = both[:half] + both[half:]
        for i in range(4):
            for second in range(2):
                grid[pl.ds(i * 16 + 2 * pair + second, channels, stride=64), :] = value[
                    i * channels : (i + 1) * channels, second * 128 : (second + 1) * 128
                ]


def forward(weights, grid, pair_grid, count, depth):
    chunk = 512

    def body(step, total):
        at = pl.multiple_of(step * chunk, chunk)
        high, low = split(grid[pl.ds(at, chunk), :])
        pair_grid[pl.ds(at, chunk), :128] = high
        pair_grid[pl.ds(at, chunk), 128:] = low
        return total + dot(weights[:, pl.ds(at, chunk)], pair_grid[pl.ds(at, chunk), :], (1, 0))

    total = lax.fori_loop(0, depth // chunk, body, jnp.zeros((2 * count, 256), F32))
    return (total[:count, :128] + total[:count, 128:]) + (total[count:, :128] + total[count:, 128:])


def kernel_grad(gradient, pair_grid, result, count, depth):
    chunk = 512
    high, low = split(gradient)
    both = jnp.concatenate(
        [jnp.concatenate([high, high], axis=1), jnp.concatenate([low, low], axis=1)], axis=0
    )

    @pl.loop(0, depth // chunk)
    def _(step):
        at = pl.multiple_of(step * chunk, chunk)
        value = dot(both, pair_grid[pl.ds(at, chunk), :], (1, 1))
        result[:, pl.ds(at, chunk)] = (value[:count] + value[count:]) * (1.0 / SAMPLES)


def column_grad(weights, gradient, grid, count, depth):
    chunk = 512
    high, low = split(gradient)
    both = jnp.concatenate(
        [jnp.concatenate([high, low], axis=1), jnp.concatenate([high, low], axis=1)], axis=0
    )

    @pl.loop(0, depth // chunk)
    def _(step):
        at = pl.multiple_of(step * chunk, chunk)
        value = dot(weights[:, pl.ds(at, chunk)], both, (0, 0))
        grid[pl.ds(at, chunk), :] = value[:, :128] + value[:, 128:]


def rows_grad(grid, spread, taps, total, channels):
    half = 4 * channels
    total[...] = jnp.zeros_like(total)

    @pl.loop(0, 8)
    def _(pair):
        for i in range(4):
            for second in range(2):
                high, low = split(grid[pl.ds(i * 16 + 2 * pair + second, channels, stride=64), :])
                lanes = slice(second * 128, (second + 1) * 128)
                taps[i * channels : (i + 1) * channels, lanes] = high
                taps[half + i * channels : half + (i + 1) * channels, lanes] = low
        both = dot(taps[...], spread[pair], (1, 0))
        total[...] += both[:half] + both[half:]


def copy_to(source, target, sends, receives, at, device):
    return pltpu.make_async_remote_copy(
        src_ref=source,
        dst_ref=target,
        send_sem=sends.at[at],
        recv_sem=receives.at[at],
        device_id=device,
        device_id_type=MESH,
    )


def layers_kernel(
    vol, cot, w1, b1, w2, b2,
    out, gw1, gw2, gbias, dvol,
    halo, hidden, pre1, dhidden, got, send_z, got_z,
    pick1, pick2, spread1, spread2,
    rows1, rows2, taps1, taps2, drows1, drows2,
    grid1, grid2, pairs1, pairs2, w1s, w2s,
    sends, receives,
):
    me = lax.axis_index("space")
    x, far = me // 2, me % 2
    barrier = pltpu.get_barrier_semaphore()
    for k in range(1, 8):
        pl.semaphore_signal(barrier, inc=1, device_id={"space": (me + k) % 8}, device_id_type=MESH)
    pl.semaphore_wait(barrier, 7)

    up = copy_to(vol.at[3], halo.at[0], sends, receives, 0, {"space": (me + 1) % 8})
    down = copy_to(vol.at[0], halo.at[1], sends, receives, 1, {"space": (me + 7) % 8})
    up.start()
    down.start()

    fill_pick(pick1, 3)
    fill_pick(pick2, 2)
    fill_spread(spread1, 3)
    fill_spread(spread2, 2)
    high, low = split(w1[...])
    w1s[:MID] = high
    w1s[MID:] = low
    high, low = split(w2[...])
    w2s[...] = jnp.concatenate([high, low], axis=0)

    def place(i, part, plane):
        high, low = split(plane)
        lanes = slice(part * 256, (part + 1) * 256)
        rows1[i * CIN : (i + 1) * CIN, lanes] = high
        rows1[4 * CIN + i * CIN : 4 * CIN + (i + 1) * CIN, lanes] = low

    for i in range(4):
        for part in range(2):
            if 0 <= 2 * part + i - 1 < 4:
                place(i, part, vol[2 * part + i - 1])
    up.wait()
    down.wait()
    place(0, 0, jnp.where(me > 0, halo[0], 0.0))
    place(3, 1, jnp.where(me < 7, halo[1], 0.0))
    columns(rows1, pick1, grid1, CIN)
    pre1[...] = forward(w1s, grid1, pairs1, MID, CIN * 64) + b1[...]
    hidden[me] = smooth(pre1[...])

    partner = 2 * x + 1 - far
    cross = copy_to(hidden.at[me], hidden.at[me], sends, receives, 2, {"space": partner})
    cross.start()
    own = []
    for k in range(1, 4):
        other = 2 * ((x + k) % 4) + far
        own.append(copy_to(hidden.at[me], hidden.at[me], sends, receives, 2 + k, {"space": other}))
        own[-1].start()
    cross.wait()
    for k in range(1, 4):
        other = 2 * ((x + k) % 4) + far
        own.append(
            copy_to(hidden.at[partner], hidden.at[partner], sends, receives, 5 + k, {"space": other})
        )
        own[-1].start()
    for copy in own:
        copy.wait()

    lane = lax.broadcasted_iota(jnp.int32, (MID, 128), 1)
    first = lane < 64
    zero = jnp.zeros((MID, 128), F32)

    def put(i, m, value):
        high, low = split(value)
        lanes = slice(m * 128, (m + 1) * 128)
        rows2[i * MID : (i + 1) * MID, lanes] = high
        rows2[4 * MID + i * MID : 4 * MID + (i + 1) * MID, lanes] = low

    for m in range(4):
        near, next_one = hidden[2 * m], hidden[2 * m + 1]
        before = hidden[2 * m - 1] if m > 0 else zero
        after = hidden[2 * m + 2] if m < 3 else zero
        put(0, m, jnp.where(first, pltpu.roll(before, 64, 1), near))
        put(1, m, jnp.where(first, near, pltpu.roll(next_one, 64, 1)))
        put(2, m, jnp.where(first, pltpu.roll(near, 64, 1), next_one))
        put(3, m, jnp.where(first, next_one, pltpu.roll(after, 64, 1)))
    columns(rows2, pick2, grid2, MID)
    pre2 = forward(w2s, grid2, pairs2, OWN, MID * 64) + b2[...]
    out[...] = smooth(pre2)
    grad2 = cot[...] * slope(pre2)
    column_grad(w2s, grad2, grid2, OWN, MID * 64)
    rows_grad(grid2, spread2, taps2, drows2, MID)

    def taken(i, m):
        if not 0 <= m < 4:
            return zero
        return drows2[i * MID : (i + 1) * MID, m * 128 : (m + 1) * 128]

    for m in range(4):
        dhidden[2 * m] = jnp.where(
            first,
            taken(1, m) + pltpu.roll(taken(3, m - 1), 64, 1),
            pltpu.roll(taken(2, m), 64, 1) + taken(0, m),
        )
        dhidden[2 * m + 1] = jnp.where(
            first,
            pltpu.roll(taken(1, m), 64, 1) + taken(3, m),
            taken(2, m) + pltpu.roll(taken(0, m + 1), 64, 1),
        )
    shares = []
    for k in range(1, 4):
        other = (x + k) % 4
        shares.append(
            copy_to(
                dhidden.at[pl.ds(2 * other, 2)], got.at[k - 1], sends, receives, 8 + k,
                {"space": 2 * other + far},
            )
        )
        shares[-1].start()
    kernel_grad(grad2, pairs2, gw2, OWN, MID * 64)
    for copy in shares:
        copy.wait()
    send_z[...] = (dhidden[partner] + got[0, 1 - far]) + (got[1, 1 - far] + got[2, 1 - far])
    cross = copy_to(send_z, got_z, sends, receives, 12, {"space": partner})
    cross.start()
    mine = (dhidden[me] + got[0, far]) + (got[1, far] + got[2, far])
    cross.wait()
    grad1 = (mine + got_z[...]) * slope(pre1[...])

    ones = jnp.ones((8, 128), BF16)

    def sums(value):
        high, low = split(value)
        rest = (value - high.astype(F32) - low.astype(F32)).astype(BF16)
        return (dot(ones, high, (1, 1)) + dot(ones, low, (1, 1)) + dot(ones, rest, (1, 1))) * (1.0 / SAMPLES)

    gbias[...] = jnp.zeros((8, 128), F32)
    gbias[:, :MID] = sums(grad1)
    gbias[:, MID : MID + OWN] = sums(grad2)
    kernel_grad(grad1, pairs1, gw1, MID, CIN * 64)
    column_grad(w1s, grad1, grid1, MID, CIN * 64)
    rows_grad(grid1, spread1, taps1, drows1, CIN)

    def back(i, part):
        return drows1[i * CIN : (i + 1) * CIN, part * 256 : (part + 1) * 256]

    dvol[0] = back(0, 0)
    dvol[1] = back(1, 0)
    dvol[2] = back(2, 0) + back(0, 1)
    dvol[3] = back(3, 0) + back(1, 1)
    dvol[4] = back(2, 1)
    dvol[5] = back(3, 1)


def layers(vol, cot, w1, b1, w2, b2):
    shape = jax.ShapeDtypeStruct
    return pl.pallas_call(
        layers_kernel,
        out_shape=(
            shape((OWN, 128), F32),
            shape((MID, CIN * 64), F32),
            shape((OWN, MID * 64), F32),
            shape((8, 128), F32),
            shape((6, CIN, 256), F32),
        ),
        in_specs=[pl.BlockSpec(memory_space=pltpu.VMEM)] * 6,
        out_specs=[pl.BlockSpec(memory_space=pltpu.VMEM)] * 5,
        scratch_shapes=[
            pltpu.VMEM((2, CIN, 256), F32),
            pltpu.VMEM((8, MID, 128), F32),
            pltpu.VMEM((MID, 128), F32),
            pltpu.VMEM((8, MID, 128), F32),
            pltpu.VMEM((3, 2, MID, 128), F32),
            pltpu.VMEM((MID, 128), F32),
            pltpu.VMEM((MID, 128), F32),
            pltpu.VMEM((8, 512, 256), BF16),
            pltpu.VMEM((8, 512, 256), BF16),
            pltpu.VMEM((8, 256, 512), BF16),
            pltpu.VMEM((8, 256, 512), BF16),
            pltpu.VMEM((8 * CIN, 512), BF16),
            pltpu.VMEM((8 * MID, 512), BF16),
            pltpu.VMEM((8 * CIN, 256), BF16),
            pltpu.VMEM((8 * MID, 256), BF16),
            pltpu.VMEM((4 * CIN, 512), F32),
            pltpu.VMEM((4 * MID, 512), F32),
            pltpu.VMEM((CIN * 64, 128), F32),
            pltpu.VMEM((MID * 64, 128), F32),
            pltpu.VMEM((CIN * 64, 256), BF16),
            pltpu.VMEM((MID * 64, 256), BF16),
            pltpu.VMEM((2 * MID, CIN * 64), BF16),
            pltpu.VMEM((2 * OWN, MID * 64), BF16),
            pltpu.SemaphoreType.DMA((13,)),
            pltpu.SemaphoreType.DMA((13,)),
        ],
        compiler_params=pltpu.CompilerParams(
            collective_id=0, has_side_effects=True, vmem_limit_bytes=48 << 20
        ),
        name="layers",
    )(vol, cot, w1, b1, w2, b2)


def flip(index, k):
    if k == 1:
        return index + 1 - 2 * (index % 2)
    if k == 2:
        return (index + 2) % 4
    return 3 - index


def reduce_kernel(
    gw1, gw2, gbias, dvol,
    tw1, tw2, tbias, tvol,
    halo, c1, c2, c3, s1, s2, s3, x1, x3, m1, m3, y1, y2, y3, n1, n2, n3,
    r1, r2, r3, o1, o2, o3, a1, a2, a3,
    sends, receives,
):
    dp, me = lax.axis_index("dp"), lax.axis_index("space")
    core, low, y = dp % 2, (dp // 2) % 8, dp // 16
    x, far = me // 2, me % 2
    run, step = 2 * far + low // 4, low % 4
    core_peer = {"dp": dp + 1 - 2 * core, "space": me}
    x_peers = [{"dp": dp, "space": 2 * flip(x, k) + far} for k in (1, 2, 3)]
    y_peers = [{"dp": flip(y, k) * 16 + dp % 16, "space": me} for k in (1, 2, 3)]
    b_peers = [
        {"dp": y * 16 + (4 * (low // 4) + flip(step, k)) * 2 + core, "space": me} for k in (1, 2, 3)
    ]
    a_peers = [
        {
            "dp": y * 16 + (4 * (flip(run, k) % 2) + step) * 2 + core,
            "space": 2 * x + flip(run, k) // 2,
        }
        for k in (1, 2, 3)
    ]
    above = {"dp": dp, "space": (me + 1) % 8}
    below = {"dp": dp, "space": (me + 7) % 8}
    barrier = pltpu.get_barrier_semaphore()
    peers = [core_peer, *x_peers, *y_peers, *b_peers, *a_peers, above, below]
    for peer in peers:
        pl.semaphore_signal(barrier, inc=1, device_id=peer, device_id_type=MESH)
    pl.semaphore_wait(barrier, len(peers))

    used = [0]

    def send(source, target, peer):
        copy = copy_to(source, target, sends, receives, used[0], peer)
        used[0] += 1
        copy.start()
        return copy

    def wait(copies):
        for copy in copies:
            copy.wait()

    lane = lax.broadcasted_iota(jnp.int32, (8, 128), 1)
    shared = lane < MID

    def rows(count, index):
        return pl.ds(pl.multiple_of(count * index, 8), count)

    def lanes(start, count):
        return pl.ds(pl.multiple_of(start, 128), count)

    edges = [send(dvol.at[0], halo.at[1], below), send(dvol.at[5], halo.at[0], above)]
    wait(
        [
            send(gw1.at[rows(32, 1 - core), :], c1, core_peer),
            send(gw2.at[:, lanes((1 - core) * 2048, 2048)], c2, core_peer),
            send(gbias, c3, core_peer),
        ]
    )
    s1[...] = gw1[rows(32, core), :] + c1[...]
    s2[...] = gw2[:, lanes(core * 2048, 2048)] + c2[...]
    s3[...] = gbias[...] + c3[...]
    copies = []
    for k in (1, 2, 3):
        copies.append(send(s1.at[rows(8, flip(x, k)), :], x1.at[k - 1], x_peers[k - 1]))
        copies.append(send(s3, x3.at[k - 1], x_peers[k - 1]))
    wait(copies)
    m1[...] = (s1[rows(8, x), :] + x1[0]) + (x1[1] + x1[2])
    m3[...] = jnp.where(shared, (s3[...] + x3[0]) + (x3[1] + x3[2]), s3[...])
    copies = []
    for k in (1, 2, 3):
        there = lanes(flip(y, k) * 512, 512)
        copies.append(send(m1.at[:, there], y1.at[k - 1], y_peers[k - 1]))
        copies.append(send(s2.at[:, there], y2.at[k - 1], y_peers[k - 1]))
        copies.append(send(m3, y3.at[k - 1], y_peers[k - 1]))
    wait(copies)
    here = lanes(y * 512, 512)
    n1[...] = (m1[:, here] + y1[0]) + (y1[1] + y1[2])
    n2[...] = (s2[:, here] + y2[0]) + (y2[1] + y2[2])
    n3[...] = (m3[...] + y3[0]) + (y3[1] + y3[2])
    copies = []
    for k in (1, 2, 3):
        there = lanes(flip(step, k) * 128, 128)
        copies.append(send(n1.at[:, there], r1.at[k - 1], b_peers[k - 1]))
        copies.append(send(n2.at[:, there], r2.at[k - 1], b_peers[k - 1]))
        copies.append(send(n3, r3.at[k - 1], b_peers[k - 1]))
    wait(copies)
    here = lanes(step * 128, 128)
    o1[...] = (n1[:, here] + r1[0]) + (r1[1] + r1[2])
    o2[...] = (n2[:, here] + r2[0]) + (r2[1] + r2[2])
    o3[...] = (n3[...] + r3[0]) + (r3[1] + r3[2])
    copies = [send(o2, a2, a_peers[0])]
    for k in (1, 2, 3):
        copies.append(send(o1, a1.at[k - 1], a_peers[k - 1]))
        copies.append(send(o3, a3.at[k - 1], a_peers[k - 1]))
    wait(copies)
    near = o3[...] + a3[0]
    tbias[...] = jnp.where(shared, near + (a3[1] + a3[2]), near)
    own_rows = rows(8, core * 4 + x)
    at1 = y * 512 + step * 128
    at2 = core * 2048 + at1
    tw1[own_rows, lanes(at1, 128)] = (o1[...] + a1[0]) + (a1[1] + a1[2])
    tw2[:, lanes(at2, 128)] = o2[...] + a2[...]
    copies = []
    for peer in b_peers:
        here1 = tw1.at[own_rows, lanes(at1, 128)]
        here2 = tw2.at[:, lanes(at2, 128)]
        copies += [send(here1, here1, peer), send(here2, here2, peer)]
    wait(copies)
    copies = []
    for peer in y_peers:
        here1 = tw1.at[own_rows, lanes(y * 512, 512)]
        here2 = tw2.at[:, lanes(core * 2048 + y * 512, 512)]
        copies += [send(here1, here1, peer), send(here2, here2, peer)]
    wait(copies)
    here2 = tw2.at[:, lanes(core * 2048, 2048)]
    last = [send(here2, here2, core_peer)]
    copies = []
    for peer in x_peers:
        here1 = tw1.at[own_rows, :]
        copies.append(send(here1, here1, peer))
    wait(copies)
    here1 = tw1.at[rows(32, core), :]
    last.append(send(here1, here1, core_peer))
    wait(edges)
    tvol[0] = dvol[1] + jnp.where(me > 0, halo[0], 0.0)
    tvol[1] = dvol[2]
    tvol[2] = dvol[3]
    tvol[3] = dvol[4] + jnp.where(me < 7, halo[1], 0.0)
    wait(last)


def reduced(gw1, gw2, gbias, dvol):
    shape = jax.ShapeDtypeStruct

    def vmem(*size):
        return pltpu.VMEM(size, F32)

    return pl.pallas_call(
        reduce_kernel,
        out_shape=(
            shape((MID, CIN * 64), F32),
            shape((OWN, MID * 64), F32),
            shape((8, 128), F32),
            shape((4, CIN, 256), F32),
        ),
        in_specs=[pl.BlockSpec(memory_space=pltpu.VMEM)] * 4,
        out_specs=[pl.BlockSpec(memory_space=pltpu.VMEM)] * 4,
        scratch_shapes=[
            vmem(2, CIN, 256),
            vmem(32, 2048), vmem(8, 2048), vmem(8, 128),
            vmem(32, 2048), vmem(8, 2048), vmem(8, 128),
            vmem(3, 8, 2048), vmem(3, 8, 128),
            vmem(8, 2048), vmem(8, 128),
            vmem(3, 8, 512), vmem(3, 8, 512), vmem(3, 8, 128),
            vmem(8, 512), vmem(8, 512), vmem(8, 128),
            vmem(3, 8, 128), vmem(3, 8, 128), vmem(3, 8, 128),
            vmem(8, 128), vmem(8, 128), vmem(8, 128),
            vmem(3, 8, 128), vmem(8, 128), vmem(3, 8, 128),
            pltpu.SemaphoreType.DMA((64,)),
            pltpu.SemaphoreType.DMA((64,)),
        ],
        compiler_params=pltpu.CompilerParams(
            collective_id=1, has_side_effects=True, vmem_limit_bytes=32 << 20
        ),
        name="reduced",
    )(gw1, gw2, gbias, dvol)


def on_device(volume, cotangent, w_first, b_first, w_second, b_second):
    vol = volume[0].transpose(1, 0, 2)
    out, gw1, gw2, gbias, dvol = layers(
        vol, cotangent[0], w_first, b_first[:, None], w_second, b_second[:, None]
    )
    gw1, gw2, gbias, dvol = reduced(gw1, gw2, gbias, dvol)
    return (
        out[None],
        dvol.transpose(1, 0, 2)[None],
        gw1,
        gbias[0, :MID],
        gw2,
        gbias[0, MID : MID + OWN],
    )


def solution(mesh):
    in_specs = (
        P("dp", None, "space", None),
        P("dp", "space", None),
        P(),
        P(),
        P("space", None),
        P("space"),
    )
    out_specs = (
        P("dp", "space", None),
        P("dp", None, "space", None),
        P(),
        P(),
        P("space", None),
        P("space"),
    )
    return jax.shard_map(
        on_device, mesh=mesh, in_specs=in_specs, out_specs=out_specs, check_vma=False
    )
```

```python
import functools

import jax
import jax.numpy as jnp
from jax import lax
from jax.experimental import pallas as pl
from jax.experimental.pallas import tpu as pltpu
from jax.sharding import PartitionSpec as P

MESH = pl.DeviceIdType.MESH
F32 = jnp.float32
BF16 = jnp.bfloat16
SLOPE = 0.3
CIN = 32
MID = 64
OWN = 8
SAMPLES = 64
UNROLL = 4


def split(value):
    high = value.astype(BF16)
    low = (value - high.astype(F32)).astype(BF16)
    return high, low


def dot(a, b, contract):
    return lax.dot_general(a, b, ((contract[:1], contract[1:]), ((), ())), preferred_element_type=F32)


def smooth(pre):
    decay = jnp.exp(-jnp.abs(pre))
    soft = jnp.maximum(pre, 0.0) + jnp.log(1.0 + decay)
    return SLOPE * pre + (1.0 - SLOPE) * soft


def slope(pre):
    decay = jnp.exp(-jnp.abs(pre))
    return SLOPE + (1.0 - SLOPE) * (jnp.where(pre >= 0.0, 1.0, decay) / (1.0 + decay))


def source_of(column, tap, log_half):
    half = 1 << log_half
    width = 2 * half
    slab = lax.shift_right_logical(column, 2 * log_half)
    row = lax.shift_right_logical(column, log_half) & (half - 1)
    cell = column & (half - 1)
    high = 2 * row + lax.shift_right_logical(tap, 2) - 1
    low = 2 * cell + (tap & 3) - 1
    inside = (high >= 0) & (high < width) & (low >= 0) & (low < width)
    return jnp.where(inside, slab * (width * width) + high * width + low, -1)


def fill_pick(pick, log_half):
    @pl.loop(0, 8)
    def _(pair):
        lane = lax.broadcasted_iota(jnp.int32, (8, 256), 1)
        source = source_of(lane & 127, 2 * pair + lax.shift_right_logical(lane, 7), log_half)
        cell = lax.broadcasted_iota(jnp.int32, (512, 256), 0)
        pick[pair] = jnp.where(cell == source[0:1], 1.0, 0.0).astype(BF16)


def fill_spread(spread, log_half):
    @pl.loop(0, 8)
    def _(pair):
        row = lax.broadcasted_iota(jnp.int32, (256, 128), 0)
        source = source_of(row & 127, 2 * pair + lax.shift_right_logical(row, 7), log_half)
        cell = lax.broadcasted_iota(jnp.int32, (256, 128), 1)
        for part in range(4):
            spread[pair, :, part * 128 : (part + 1) * 128] = jnp.where(
                cell + part * 128 == source, 1.0, 0.0
            ).astype(BF16)


def columns(rows, pick, grid, channels):
    half = 4 * channels

    @pl.loop(0, 8, unroll=UNROLL)
    def _(pair):
        both = dot(rows[...], pick[pair], (1, 0))
        value = both[:half] + both[half:]
        for i in range(4):
            for second in range(2):
                grid[pl.ds(i * 16 + 2 * pair + second, channels, stride=64), :] = value[
                    i * channels : (i + 1) * channels, second * 128 : (second + 1) * 128
                ]


def forward(weights, grid, pair_grid, count, depth):
    chunk = 512

    def body(step, total):
        at = pl.multiple_of(step * chunk, chunk)
        high, low = split(grid[pl.ds(at, chunk), :])
        pair_grid[pl.ds(at, chunk), :128] = high
        pair_grid[pl.ds(at, chunk), 128:] = low
        return total + dot(weights[:, pl.ds(at, chunk)], pair_grid[pl.ds(at, chunk), :], (1, 0))

    total = lax.fori_loop(0, depth // chunk, body, jnp.zeros((2 * count, 256), F32), unroll=UNROLL)
    return (total[:count, :128] + total[:count, 128:]) + (total[count:, :128] + total[count:, 128:])


def kernel_grad(gradient, pair_grid, result, count, depth):
    chunk = 512
    high, low = split(gradient)
    both = jnp.concatenate(
        [jnp.concatenate([high, high], axis=1), jnp.concatenate([low, low], axis=1)], axis=0
    )

    @pl.loop(0, depth // chunk, unroll=UNROLL)
    def _(step):
        at = pl.multiple_of(step * chunk, chunk)
        value = dot(both, pair_grid[pl.ds(at, chunk), :], (1, 1))
        result[:, pl.ds(at, chunk)] = (value[:count] + value[count:]) * (1.0 / SAMPLES)


def column_grad(weights, gradient, grid, count, depth):
    chunk = 512
    high, low = split(gradient)
    both = jnp.concatenate(
        [jnp.concatenate([high, low], axis=1), jnp.concatenate([high, low], axis=1)], axis=0
    )

    @pl.loop(0, depth // chunk, unroll=UNROLL)
    def _(step):
        at = pl.multiple_of(step * chunk, chunk)
        value = dot(weights[:, pl.ds(at, chunk)], both, (0, 0))
        grid[pl.ds(at, chunk), :] = value[:, :128] + value[:, 128:]


def rows_grad(grid, spread, taps, total, channels):
    half = 4 * channels
    total[...] = jnp.zeros_like(total)

    @pl.loop(0, 8, unroll=UNROLL)
    def _(pair):
        for i in range(4):
            for second in range(2):
                high, low = split(grid[pl.ds(i * 16 + 2 * pair + second, channels, stride=64), :])
                lanes = slice(second * 128, (second + 1) * 128)
                taps[i * channels : (i + 1) * channels, lanes] = high
                taps[half + i * channels : half + (i + 1) * channels, lanes] = low
        both = dot(taps[...], spread[pair], (1, 0))
        total[...] += both[:half] + both[half:]


def fill_fold(fold):
    @pl.loop(0, 8)
    def _(pair):
        row = lax.broadcasted_iota(jnp.int32, (128, 128), 0)
        cell = source_of(row & 15, 2 * pair + lax.shift_right_logical(row, 6), 2)
        plane = lax.shift_right_logical(row, 5) & 1
        lane = lax.broadcasted_iota(jnp.int32, (128, 128), 1)
        fold[pair] = jnp.where((cell >= 0) & (lane == plane * 64 + cell), 1.0, 0.0).astype(BF16)


def own_columns(weights, gradient, me, grid, depth):
    chunk = 512
    lane = lax.broadcasted_iota(jnp.int32, (MID, 128), 1)
    near = pltpu.roll(gradient, (144 - 16 * me) % 128, 1)
    again = pltpu.roll(gradient, (176 - 16 * me) % 128, 1)
    chosen = jnp.where(lane < 48, near, again)
    outside = ((lane < 16) & (me == 0)) | ((lane >= 32) & (lane < 48) & (me == 7))
    high, low = split(jnp.where(outside, 0.0, chosen))
    packed = jnp.where(lane < 64, high.astype(F32), pltpu.roll(low.astype(F32), 64, 1)).astype(BF16)
    both = jnp.concatenate([packed, packed], axis=0)

    @pl.loop(0, depth // chunk, unroll=UNROLL)
    def _(step):
        at = pl.multiple_of(step * chunk, chunk)
        value = dot(weights[:, pl.ds(at, chunk)], both, (0, 0))
        grid[pl.ds(at, chunk), :] = value + pltpu.roll(value, 64, 1)


def own_planes(grid, fold, taps):
    lane = lax.broadcasted_iota(jnp.int32, (MID, 128), 1)
    slot = lax.shift_right_logical(lane, 4)

    def body(pair, total):
        value = jnp.zeros((MID, 128), F32)
        for second in range(2):
            for order, i in enumerate((3, 1, 0, 2)):
                part = grid[pl.ds(i * 16 + 2 * pair + second, MID, stride=64), :]
                value = jnp.where(slot == 4 * second + order, part, value)
        high, low = split(value)
        taps[pair, :MID] = high
        taps[pair, MID:] = low
        return total + dot(taps[pair], fold[pair], (1, 0))

    total = lax.fori_loop(0, 8, body, jnp.zeros((2 * MID, 128), F32), unroll=UNROLL)
    return total[:MID] + total[MID:]


def copy_to(source, target, sends, receives, at, device):
    return pltpu.make_async_remote_copy(
        src_ref=source,
        dst_ref=target,
        send_sem=sends.at[at],
        recv_sem=receives.at[at],
        device_id=device,
        device_id_type=MESH,
    )


def flip(index, k):
    if k == 1:
        return index + 1 - 2 * (index % 2)
    if k == 2:
        return (index + 2) % 4
    return 3 - index


def step_kernel(
    vol_in, cot_in, w1_in, b1, w2_in, b2,
    out, tw1, tw2, tbias, tvol,
    raw, planes, halo, hidden, pre1, pre2, grad2, w1, w2, bias2,
    pick1, pick2, spread1, fold,
    rows1, rows2, taps1, taps2, drows1,
    grid1, grid2, pairs1, pairs2, w1s, w2s,
    gw1, gw2, gbias, edge_out, edge_in, inner,
    c1, c2, c3, s1, s2, s3, x1, x3, m1, m3, y1, y2, y3, n1, n2, n3,
    r1, r2, r3, o1, o2, o3, a1, a2, a3,
    loads, sends, receives,
):
    dp, me = lax.axis_index("dp"), lax.axis_index("space")
    core, low, y = dp % 2, (dp // 2) % 8, dp // 16
    x, far = me // 2, me % 2
    run, step = 2 * far + low // 4, low % 4
    partner = 2 * x + 1 - far
    core_peer = {"dp": dp + 1 - 2 * core, "space": me}
    z_peer = {"dp": dp, "space": partner}
    mirror = {"dp": y * 16 + (7 - low) * 2 + core, "space": partner}
    x_peers = [{"dp": dp, "space": 2 * flip(x, k) + far} for k in (1, 2, 3)]
    y_peers = [{"dp": flip(y, k) * 16 + dp % 16, "space": me} for k in (1, 2, 3)]
    b_peers = [
        {"dp": y * 16 + (4 * (low // 4) + flip(step, k)) * 2 + core, "space": me} for k in (1, 2, 3)
    ]
    a_peers = [
        {
            "dp": y * 16 + (4 * (flip(run, k) % 2) + step) * 2 + core,
            "space": 2 * x + flip(run, k) // 2,
        }
        for k in (1, 2, 3)
    ]
    space_peers = [{"dp": dp, "space": (me + k) % 8} for k in range(1, 8)]
    above, below = space_peers[0], space_peers[6]
    barrier = pltpu.get_barrier_semaphore()
    peers = [*space_peers, core_peer, mirror, *y_peers, *b_peers, *a_peers]
    for peer in peers:
        pl.semaphore_signal(barrier, inc=1, device_id=peer, device_id_type=MESH)

    used = [0]

    def send(source, target, peer):
        copy = copy_to(source, target, sends, receives, used[0], peer)
        used[0] += 1
        copy.start()
        return copy

    def wait(copies):
        for copy in copies:
            copy.wait()

    def rows(count, index):
        return pl.ds(pl.multiple_of(count * index, 8), count)

    def lanes(start, count):
        return pl.ds(pl.multiple_of(start, 128), count)

    fetches = [
        pltpu.make_async_copy(vol_in, raw, loads.at[0]),
        pltpu.make_async_copy(cot_in, hidden.at[me, MID:], loads.at[1]),
        pltpu.make_async_copy(w2_in.at[:, lanes(core * 2048, 2048)], w2.at[core, me], loads.at[2]),
        pltpu.make_async_copy(w1_in, w1, loads.at[3]),
    ]
    for fetch in fetches:
        fetch.start()
    bias2[me] = jnp.broadcast_to(b2[...], (OWN, 128))
    fetches[0].wait()
    for p in range(4):
        planes[p] = raw[:, p, :]
    fill_pick(pick1, 3)
    fetches[1].wait()
    fetches[2].wait()
    pl.semaphore_wait(barrier, len(peers))

    edges = [send(planes.at[3], halo.at[0], above), send(planes.at[0], halo.at[1], below)]
    mine = w2.at[core, me]
    cross_w = [send(mine, mine, mirror), send(bias2.at[me], bias2.at[me], mirror)]
    own_w = []
    for peer in x_peers:
        own_w += [send(mine, mine, peer), send(bias2.at[me], bias2.at[me], peer)]

    def place(i, part, plane):
        high, low_part = split(plane)
        at = slice(part * 256, (part + 1) * 256)
        rows1[i * CIN : (i + 1) * CIN, at] = high
        rows1[4 * CIN + i * CIN : 4 * CIN + (i + 1) * CIN, at] = low_part

    for i in range(4):
        for part in range(2):
            if 0 <= 2 * part + i - 1 < 4:
                place(i, part, planes[2 * part + i - 1])
    fetches[3].wait()
    high, low_part = split(w1[...])
    w1s[:MID] = high
    w1s[MID:] = low_part
    fill_pick(pick2, 2)
    wait(edges)
    place(0, 0, jnp.where(me > 0, halo[0], 0.0))
    place(3, 1, jnp.where(me < 7, halo[1], 0.0))
    columns(rows1, pick1, grid1, CIN)
    pre1[...] = forward(w1s, grid1, pairs1, MID, CIN * 64) + b1[...]
    hidden[me, :MID] = smooth(pre1[...])

    mine = hidden.at[me]
    cross = send(mine, mine, z_peer)
    own = [send(mine, mine, peer) for peer in x_peers]
    wait(cross_w)
    other, other_bias = w2.at[core, partner], bias2.at[partner]
    for peer in x_peers:
        own_w += [send(other, other, peer), send(other_bias, other_bias, peer)]
    fill_fold(fold)
    fill_spread(spread1, 3)
    cross.wait()
    other = hidden.at[partner]
    own += [send(other, other, peer) for peer in x_peers]
    wait(own_w)
    half = w2.at[core]
    share = send(half, half, core_peer)

    def take_weights(part):
        for s in range(8):
            high, low_part = split(w2[part, s])
            at = lanes(part * 2048, 2048)
            w2s[s * OWN : (s + 1) * OWN, at] = high
            w2s[MID + s * OWN : MID + (s + 1) * OWN, at] = low_part

    take_weights(core)
    wait(own)

    lane = lax.broadcasted_iota(jnp.int32, (MID, 128), 1)
    first = lane < 64
    zero = jnp.zeros((MID, 128), F32)

    def put(i, m, value):
        high, low_part = split(value)
        at = slice(m * 128, (m + 1) * 128)
        rows2[i * MID : (i + 1) * MID, at] = high
        rows2[4 * MID + i * MID : 4 * MID + (i + 1) * MID, at] = low_part

    for m in range(4):
        near, next_one = hidden[2 * m, :MID], hidden[2 * m + 1, :MID]
        before = hidden[2 * m - 1, :MID] if m > 0 else zero
        after = hidden[2 * m + 2, :MID] if m < 3 else zero
        put(0, m, jnp.where(first, pltpu.roll(before, 64, 1), near))
        put(1, m, jnp.where(first, near, pltpu.roll(next_one, 64, 1)))
        put(2, m, jnp.where(first, pltpu.roll(near, 64, 1), next_one))
        put(3, m, jnp.where(first, next_one, pltpu.roll(after, 64, 1)))
    columns(rows2, pick2, grid2, MID)
    share.wait()
    take_weights(1 - core)
    total = forward(w2s, grid2, pairs2, MID, MID * 64)
    for s in range(8):
        block = slice(s * OWN, (s + 1) * OWN)
        value = total[block] + bias2[s]
        pre2[s] = value
        grad2[s] = hidden[s, MID:] * slope(value)
    all_grad2 = jnp.concatenate([grad2[s] for s in range(8)], axis=0)
    own_columns(w2s, all_grad2, me, grid2, MID * 64)
    grad1 = own_planes(grid2, fold, taps2) * slope(pre1[...])
    kernel_grad(grad1, pairs1, gw1, MID, CIN * 64)
    copies = [send(gw1.at[rows(32, 1 - core), :], c1, core_peer)]

    ones = jnp.ones((8, 128), BF16)

    def sums(value):
        high, low_part = split(value)
        rest = (value - high.astype(F32) - low_part.astype(F32)).astype(BF16)
        return (dot(ones, high, (1, 1)) + dot(ones, low_part, (1, 1)) + dot(ones, rest, (1, 1))) * (
            1.0 / SAMPLES
        )

    own_grad2 = grad2[me]
    gbias[...] = jnp.zeros((8, 128), F32)
    gbias[:, :MID] = sums(grad1)
    gbias[:, MID : MID + OWN] = sums(own_grad2)
    copies.append(send(gbias, c3, core_peer))
    wait(copies)
    s1[...] = gw1[rows(32, core), :] + c1[...]
    s3[...] = gbias[...] + c3[...]
    copies = []
    for k in (1, 2, 3):
        copies.append(send(s1.at[rows(8, flip(x, k)), :], x1.at[k - 1], x_peers[k - 1]))
        copies.append(send(s3, x3.at[k - 1], x_peers[k - 1]))
    kernel_grad(own_grad2, pairs2, gw2, OWN, MID * 64)
    early = send(gw2.at[:, lanes((1 - core) * 2048, 2048)], c2, core_peer)
    out[...] = smooth(pre2[me])
    column_grad(w1s, grad1, grid1, MID, CIN * 64)
    early.wait()
    s2[...] = gw2[:, lanes(core * 2048, 2048)] + c2[...]
    wait(copies)
    shared = lax.broadcasted_iota(jnp.int32, (8, 128), 1) < MID
    m1[...] = (s1[rows(8, x), :] + x1[0]) + (x1[1] + x1[2])
    m3[...] = jnp.where(shared, (s3[...] + x3[0]) + (x3[1] + x3[2]), s3[...])
    copies = []
    for k in (1, 2, 3):
        there = lanes(flip(y, k) * 512, 512)
        copies.append(send(m1.at[:, there], y1.at[k - 1], y_peers[k - 1]))
        copies.append(send(s2.at[:, there], y2.at[k - 1], y_peers[k - 1]))
        copies.append(send(m3, y3.at[k - 1], y_peers[k - 1]))
    rows_grad(grid1, spread1, taps1, drows1, CIN)
    wait(copies)
    here = lanes(y * 512, 512)
    n1[...] = (m1[:, here] + y1[0]) + (y1[1] + y1[2])
    n2[...] = (s2[:, here] + y2[0]) + (y2[1] + y2[2])
    n3[...] = (m3[...] + y3[0]) + (y3[1] + y3[2])
    copies = []
    for k in (1, 2, 3):
        there = lanes(flip(step, k) * 128, 128)
        copies.append(send(n1.at[:, there], r1.at[k - 1], b_peers[k - 1]))
        copies.append(send(n2.at[:, there], r2.at[k - 1], b_peers[k - 1]))
        copies.append(send(n3, r3.at[k - 1], b_peers[k - 1]))

    def back(i, part):
        return drows1[i * CIN : (i + 1) * CIN, part * 256 : (part + 1) * 256]

    edge_out[0] = back(0, 0)
    edge_out[1] = back(3, 1)
    edges = [send(edge_out.at[0], edge_in.at[1], below), send(edge_out.at[1], edge_in.at[0], above)]
    wait(copies)
    here = lanes(step * 128, 128)
    o1[...] = (n1[:, here] + r1[0]) + (r1[1] + r1[2])
    o2[...] = (n2[:, here] + r2[0]) + (r2[1] + r2[2])
    o3[...] = (n3[...] + r3[0]) + (r3[1] + r3[2])
    copies = []
    for k in (1, 2, 3):
        copies.append(send(o1, a1.at[k - 1], a_peers[k - 1]))
        copies.append(send(o3, a3.at[k - 1], a_peers[k - 1]))
    copies.append(send(o2, a2, a_peers[0]))
    tvol[:, 1, :] = back(2, 0) + back(0, 1)
    tvol[:, 2, :] = back(3, 0) + back(1, 1)
    inner[0] = back(1, 0)
    inner[1] = back(2, 1)
    wait(copies)
    near = o3[...] + a3[0]
    tbias[...] = jnp.where(shared, near + (a3[1] + a3[2]), near)
    own_rows = rows(8, core * 4 + x)
    at1 = y * 512 + step * 128
    at2 = core * 2048 + at1
    tw1[own_rows, lanes(at1, 128)] = (o1[...] + a1[0]) + (a1[1] + a1[2])
    tw2[:, lanes(at2, 128)] = o2[...] + a2[...]
    copies = []
    for peer in b_peers:
        here1 = tw1.at[own_rows, lanes(at1, 128)]
        here2 = tw2.at[:, lanes(at2, 128)]
        copies += [send(here1, here1, peer), send(here2, here2, peer)]
    wait(edges)
    tvol[:, 0, :] = inner[0] + jnp.where(me > 0, edge_in[0], 0.0)
    tvol[:, 3, :] = inner[1] + jnp.where(me < 7, edge_in[1], 0.0)
    wait(copies)
    copies = []
    for peer in y_peers:
        here1 = tw1.at[own_rows, lanes(y * 512, 512)]
        here2 = tw2.at[:, lanes(core * 2048 + y * 512, 512)]
        copies += [send(here1, here1, peer), send(here2, here2, peer)]
    wait(copies)
    here2 = tw2.at[:, lanes(core * 2048, 2048)]
    last = [send(here2, here2, core_peer)]
    here1 = tw1.at[own_rows, :]
    copies = [send(here1, here1, peer) for peer in x_peers]
    last.append(send(here1, here1, core_peer))
    for k, copy in zip((1, 2, 3), copies):
        copy.wait()
        here1 = tw1.at[rows(8, core * 4 + flip(x, k)), :]
        last.append(send(here1, here1, core_peer))
    wait(last)


def stepped(vol, cot, w1, b1, w2, b2):
    shape = jax.ShapeDtypeStruct

    def vmem(*size):
        return pltpu.VMEM(size, F32)

    def half(*size):
        return pltpu.VMEM(size, BF16)

    return pl.pallas_call(
        step_kernel,
        out_shape=(
            shape((OWN, 128), F32),
            shape((MID, CIN * 64), F32),
            shape((OWN, MID * 64), F32),
            shape((8, 128), F32),
            shape((CIN, 4, 256), F32),
        ),
        in_specs=[
            pl.BlockSpec(memory_space=pltpu.HBM),
            pl.BlockSpec(memory_space=pltpu.HBM),
            pl.BlockSpec(memory_space=pltpu.HBM),
            pl.BlockSpec(memory_space=pltpu.VMEM),
            pl.BlockSpec(memory_space=pltpu.HBM),
            pl.BlockSpec(memory_space=pltpu.VMEM),
        ],
        out_specs=[pl.BlockSpec(memory_space=pltpu.VMEM)] * 5,
        scratch_shapes=[
            vmem(CIN, 4, 256), vmem(4, CIN, 256), vmem(2, CIN, 256),
            vmem(8, MID + OWN, 128), vmem(MID, 128), vmem(8, OWN, 128), vmem(8, OWN, 128),
            vmem(MID, CIN * 64), vmem(2, 8, OWN, 2048), vmem(8, OWN, 128),
            half(8, 512, 256), half(8, 512, 256), half(8, 256, 512), half(8, 128, 128),
            half(8 * CIN, 512), half(8 * MID, 512), half(8 * CIN, 256), half(8, 2 * MID, 128),
            vmem(4 * CIN, 512),
            vmem(CIN * 64, 128), vmem(MID * 64, 128), half(CIN * 64, 256), half(MID * 64, 256),
            half(2 * MID, CIN * 64), half(2 * MID, MID * 64),
            vmem(MID, CIN * 64), vmem(OWN, MID * 64), vmem(8, 128),
            vmem(2, CIN, 256), vmem(2, CIN, 256), vmem(2, CIN, 256),
            vmem(32, 2048), vmem(8, 2048), vmem(8, 128),
            vmem(32, 2048), vmem(8, 2048), vmem(8, 128),
            vmem(3, 8, 2048), vmem(3, 8, 128),
            vmem(8, 2048), vmem(8, 128),
            vmem(3, 8, 512), vmem(3, 8, 512), vmem(3, 8, 128),
            vmem(8, 512), vmem(8, 512), vmem(8, 128),
            vmem(3, 8, 128), vmem(3, 8, 128), vmem(3, 8, 128),
            vmem(8, 128), vmem(8, 128), vmem(8, 128),
            vmem(3, 8, 128), vmem(8, 128), vmem(3, 8, 128),
            pltpu.SemaphoreType.DMA((4,)),
            pltpu.SemaphoreType.DMA((96,)),
            pltpu.SemaphoreType.DMA((96,)),
        ],
        compiler_params=pltpu.CompilerParams(
            collective_id=0, has_side_effects=True, vmem_limit_bytes=60 << 20
        ),
        name="stepped",
    )(vol, cot, w1, b1, w2, b2)


def finish_kernel(out, gw1, gw2, gbias, gvol, to_out, to_w1, to_w2, to_b1, to_b2, to_vol, done):
    copies = [
        pltpu.make_async_copy(source, target, done.at[at])
        for at, (source, target) in enumerate(
            [(gw1, to_w1), (gw2, to_w2), (gvol, to_vol), (out, to_out)]
        )
    ]
    for copy in copies:
        copy.start()
    to_b1[...] = gbias[0, :MID]
    to_b2[...] = gbias[0, MID : MID + OWN]
    for copy in copies:
        copy.wait()


def finished(out, gw1, gw2, gbias, gvol):
    shape = jax.ShapeDtypeStruct
    anywhere = pl.BlockSpec(memory_space=pltpu.HBM)
    vmem = pl.BlockSpec(memory_space=pltpu.VMEM)
    return pl.pallas_call(
        finish_kernel,
        out_shape=(
            shape((OWN, 128), F32),
            shape((MID, CIN * 64), F32),
            shape((OWN, MID * 64), F32),
            shape((MID,), F32),
            shape((OWN,), F32),
            shape((CIN, 4, 256), F32),
        ),
        in_specs=[vmem] * 5,
        out_specs=[anywhere, anywhere, anywhere, vmem, vmem, anywhere],
        scratch_shapes=[pltpu.SemaphoreType.DMA((4,))],
        name="finished",
    )(out, gw1, gw2, gbias, gvol)


def on_device(volume, cotangent, w_first, b_first, w_second, b_second):
    results = stepped(
        volume[0], cotangent[0], w_first, b_first[:, None], w_second, b_second[:, None]
    )
    out, gw1, gw2, gb1, gb2, gvol = finished(*results)
    return (out[None], gvol[None], gw1, gb1, gw2, gb2)


def solution(mesh):
    in_specs = (
        P("dp", None, "space", None),
        P("dp", "space", None),
        P(),
        P(),
        P("space", None),
        P("space"),
    )
    out_specs = (
        P("dp", "space", None),
        P("dp", None, "space", None),
        P(),
        P(),
        P("space", None),
        P("space"),
    )
    return jax.shard_map(
        on_device, mesh=mesh, in_specs=in_specs, out_specs=out_specs, check_vma=False
    )
```

```python
import functools

import jax
import jax.numpy as jnp
from jax import lax
from jax.experimental import pallas as pl
from jax.experimental.pallas import tpu as pltpu
from jax.sharding import PartitionSpec as P

MESH = pl.DeviceIdType.MESH
F32 = jnp.float32
BF16 = jnp.bfloat16
SLOPE = 0.3
CIN = 32
MID = 64
OWN = 8
SAMPLES = 64
UNROLL = 4


def split(value):
    high = value.astype(BF16)
    low = (value - high.astype(F32)).astype(BF16)
    return high, low


def dot(a, b, contract):
    return lax.dot_general(a, b, ((contract[:1], contract[1:]), ((), ())), preferred_element_type=F32)


def smooth(pre):
    decay = jnp.exp(-jnp.abs(pre))
    soft = jnp.maximum(pre, 0.0) + jnp.log(1.0 + decay)
    return SLOPE * pre + (1.0 - SLOPE) * soft


def slope(pre):
    decay = jnp.exp(-jnp.abs(pre))
    return SLOPE + (1.0 - SLOPE) * (jnp.where(pre >= 0.0, 1.0, decay) / (1.0 + decay))


def source_of(column, tap, log_half):
    half = 1 << log_half
    width = 2 * half
    slab = lax.shift_right_logical(column, 2 * log_half)
    row = lax.shift_right_logical(column, log_half) & (half - 1)
    cell = column & (half - 1)
    high = 2 * row + lax.shift_right_logical(tap, 2) - 1
    low = 2 * cell + (tap & 3) - 1
    inside = (high >= 0) & (high < width) & (low >= 0) & (low < width)
    return jnp.where(inside, slab * (width * width) + high * width + low, -1)


def fill_pick(pick, log_half):
    @pl.loop(0, 8)
    def _(pair):
        lane = lax.broadcasted_iota(jnp.int32, (8, 256), 1)
        source = source_of(lane & 127, 2 * pair + lax.shift_right_logical(lane, 7), log_half)
        cell = lax.broadcasted_iota(jnp.int32, (512, 256), 0)
        pick[pair] = jnp.where(cell == source[0:1], 1.0, 0.0).astype(BF16)


def fill_spread(spread, log_half):
    @pl.loop(0, 8)
    def _(pair):
        row = lax.broadcasted_iota(jnp.int32, (256, 128), 0)
        source = source_of(row & 127, 2 * pair + lax.shift_right_logical(row, 7), log_half)
        cell = lax.broadcasted_iota(jnp.int32, (256, 128), 1)
        for part in range(4):
            spread[pair, :, part * 128 : (part + 1) * 128] = jnp.where(
                cell + part * 128 == source, 1.0, 0.0
            ).astype(BF16)


def columns(rows, pick, grid, channels):
    half = 4 * channels

    @pl.loop(0, 8, unroll=UNROLL)
    def _(pair):
        both = dot(rows[...], pick[pair], (1, 0))
        value = both[:half] + both[half:]
        for i in range(4):
            for second in range(2):
                grid[pl.ds(i * 16 + 2 * pair + second, channels, stride=64), :] = value[
                    i * channels : (i + 1) * channels, second * 128 : (second + 1) * 128
                ]


def forward(weights, grid, pair_grid, count, depth):
    chunk = 512

    def body(step, total):
        at = pl.multiple_of(step * chunk, chunk)
        high, low = split(grid[pl.ds(at, chunk), :])
        pair_grid[pl.ds(at, chunk), :128] = high
        pair_grid[pl.ds(at, chunk), 128:] = low
        return total + dot(weights[:, pl.ds(at, chunk)], pair_grid[pl.ds(at, chunk), :], (1, 0))

    total = lax.fori_loop(0, depth // chunk, body, jnp.zeros((2 * count, 256), F32), unroll=UNROLL)
    return (total[:count, :128] + total[:count, 128:]) + (total[count:, :128] + total[count:, 128:])


def kernel_grad(gradient, pair_grid, result, count, depth):
    chunk = 512
    high, low = split(gradient)
    both = jnp.concatenate(
        [jnp.concatenate([high, high], axis=1), jnp.concatenate([low, low], axis=1)], axis=0
    )

    @pl.loop(0, depth // chunk, unroll=UNROLL)
    def _(step):
        at = pl.multiple_of(step * chunk, chunk)
        value = dot(both, pair_grid[pl.ds(at, chunk), :], (1, 1))
        result[:, pl.ds(at, chunk)] = (value[:count] + value[count:]) * (1.0 / SAMPLES)


def column_grad(weights, gradient, grid, count, depth):
    chunk = 512
    high, low = split(gradient)
    both = jnp.concatenate(
        [jnp.concatenate([high, low], axis=1), jnp.concatenate([high, low], axis=1)], axis=0
    )

    @pl.loop(0, depth // chunk, unroll=UNROLL)
    def _(step):
        at = pl.multiple_of(step * chunk, chunk)
        value = dot(weights[:, pl.ds(at, chunk)], both, (0, 0))
        grid[pl.ds(at, chunk), :] = value[:, :128] + value[:, 128:]


def rows_grad(grid, spread, taps, total, channels):
    half = 4 * channels
    total[...] = jnp.zeros_like(total)

    @pl.loop(0, 8, unroll=UNROLL)
    def _(pair):
        for i in range(4):
            for second in range(2):
                high, low = split(grid[pl.ds(i * 16 + 2 * pair + second, channels, stride=64), :])
                lanes = slice(second * 128, (second + 1) * 128)
                taps[i * channels : (i + 1) * channels, lanes] = high
                taps[half + i * channels : half + (i + 1) * channels, lanes] = low
        both = dot(taps[...], spread[pair], (1, 0))
        total[...] += both[:half] + both[half:]


def fill_fold(fold):
    @pl.loop(0, 8)
    def _(pair):
        row = lax.broadcasted_iota(jnp.int32, (128, 128), 0)
        cell = source_of(row & 15, 2 * pair + lax.shift_right_logical(row, 6), 2)
        plane = lax.shift_right_logical(row, 5) & 1
        lane = lax.broadcasted_iota(jnp.int32, (128, 128), 1)
        fold[pair] = jnp.where((cell >= 0) & (lane == plane * 64 + cell), 1.0, 0.0).astype(BF16)


def own_columns(weights, gradient, me, grid, depth):
    chunk = 512
    lane = lax.broadcasted_iota(jnp.int32, (MID, 128), 1)
    near = pltpu.roll(gradient, (144 - 16 * me) % 128, 1)
    again = pltpu.roll(gradient, (176 - 16 * me) % 128, 1)
    chosen = jnp.where(lane < 48, near, again)
    outside = ((lane < 16) & (me == 0)) | ((lane >= 32) & (lane < 48) & (me == 7))
    high, low = split(jnp.where(outside, 0.0, chosen))
    packed = jnp.where(lane < 64, high.astype(F32), pltpu.roll(low.astype(F32), 64, 1)).astype(BF16)
    both = jnp.concatenate([packed, packed], axis=0)

    @pl.loop(0, depth // chunk, unroll=UNROLL)
    def _(step):
        at = pl.multiple_of(step * chunk, chunk)
        value = dot(weights[:, pl.ds(at, chunk)], both, (0, 0))
        grid[pl.ds(at, chunk), :] = value + pltpu.roll(value, 64, 1)


def own_planes(grid, fold, taps):
    lane = lax.broadcasted_iota(jnp.int32, (MID, 128), 1)
    slot = lax.shift_right_logical(lane, 4)

    def body(pair, total):
        value = jnp.zeros((MID, 128), F32)
        for second in range(2):
            for order, i in enumerate((3, 1, 0, 2)):
                part = grid[pl.ds(i * 16 + 2 * pair + second, MID, stride=64), :]
                value = jnp.where(slot == 4 * second + order, part, value)
        high, low = split(value)
        taps[pair, :MID] = high
        taps[pair, MID:] = low
        return total + dot(taps[pair], fold[pair], (1, 0))

    total = lax.fori_loop(0, 8, body, jnp.zeros((2 * MID, 128), F32), unroll=UNROLL)
    return total[:MID] + total[MID:]


def copy_to(source, target, sends, receives, at, device):
    return pltpu.make_async_remote_copy(
        src_ref=source,
        dst_ref=target,
        send_sem=sends.at[at],
        recv_sem=receives.at[at],
        device_id=device,
        device_id_type=MESH,
    )


def flip(index, k):
    if k == 0:
        return index
    if k == 1:
        return index + 1 - 2 * (index % 2)
    if k == 2:
        return (index + 2) % 4
    return 3 - index


def step_kernel(
    vol_in, cot_in, w1_in, b1_in, w2_in, b2_in,
    out, tw1, tw2, tbias, tvol,
    raw, planes, halo, hidden, pre1, pre2, grad2, w1, w2, bias1, bias2, row1, row2,
    pick1, pick2, spread1, fold,
    rows1, rows2, taps1, taps2, drows1,
    grid1, grid2, pairs1, pairs2, w1s, w2s,
    grad1, gw1, gw1_own, gw2, gbias, edge_out, edge_in, inner,
    c1, c2, c3, s1, s2, s3, xy1, x3, m3, y2, y3, n1, n2, n3,
    r1, r2, r3, o1, o2, o3, a1, a2, a3,
    loads, sends, receives,
):
    dp, me = lax.axis_index("dp"), lax.axis_index("space")
    core, low, y = dp % 2, (dp // 2) % 8, dp // 16
    x, far = me // 2, me % 2
    run, step = 2 * far + low // 4, low % 4
    partner = 2 * x + 1 - far
    core_peer = {"dp": dp + 1 - 2 * core, "space": me}
    z_peer = {"dp": dp, "space": partner}
    mirror = {"dp": y * 16 + (7 - low) * 2 + core, "space": partner}
    x_peers = [{"dp": dp, "space": 2 * flip(x, k) + far} for k in (1, 2, 3)]
    y_peers = [{"dp": flip(y, k) * 16 + dp % 16, "space": me} for k in (1, 2, 3)]
    xy_peers = {
        (i, j): {"dp": flip(y, j) * 16 + dp % 16, "space": 2 * flip(x, i) + far}
        for i in range(4)
        for j in range(4)
        if i or j
    }
    b_peers = [
        {"dp": y * 16 + (4 * (low // 4) + flip(step, k)) * 2 + core, "space": me} for k in (1, 2, 3)
    ]
    a_peers = [
        {
            "dp": y * 16 + (4 * (flip(run, k) % 2) + step) * 2 + core,
            "space": 2 * x + flip(run, k) // 2,
        }
        for k in (1, 2, 3)
    ]
    space_peers = [{"dp": dp, "space": (me + k) % 8} for k in range(1, 8)]
    above, below = space_peers[0], space_peers[6]
    barrier = pltpu.get_barrier_semaphore()
    peers = [*space_peers, core_peer, mirror, *b_peers, *a_peers]
    peers += [peer for (_, j), peer in xy_peers.items() if j]
    for peer in peers:
        pl.semaphore_signal(barrier, inc=1, device_id=peer, device_id_type=MESH)

    used = [0]

    def send(source, target, peer):
        copy = copy_to(source, target, sends, receives, used[0], peer)
        used[0] += 1
        copy.start()
        return copy

    def wait(copies):
        for copy in copies:
            copy.wait()

    def rows(count, index):
        return pl.ds(pl.multiple_of(count * index, 8), count)

    def lanes(start, count):
        return pl.ds(pl.multiple_of(start, 128), count)

    fetches = [
        pltpu.make_async_copy(vol_in, raw, loads.at[0]),
        pltpu.make_async_copy(cot_in, hidden.at[me, MID:], loads.at[1]),
        pltpu.make_async_copy(
            w2_in.at[:, lanes(core * 2048 + y * 512, 512)], w2.at[core, y, me], loads.at[2]
        ),
        pltpu.make_async_copy(w1_in, w1, loads.at[3]),
        pltpu.make_async_copy(b1_in, row1, loads.at[4]),
        pltpu.make_async_copy(b2_in, row2, loads.at[5]),
    ]
    for fetch in fetches:
        fetch.start()

    def as_column(row, count):
        down = lax.broadcasted_iota(jnp.int32, (count, count), 0)
        along = lax.broadcasted_iota(jnp.int32, (count, count), 1)
        diagonal = jnp.where(down == along, jnp.broadcast_to(row, (count, count)), 0.0)
        return jnp.broadcast_to(jnp.sum(diagonal, axis=1, keepdims=True), (count, 128))

    fetches[0].wait()
    planes[0] = raw[:, 0, :]
    planes[3] = raw[:, 3, :]
    pl.semaphore_wait(barrier, len(peers))

    edges = [send(planes.at[3], halo.at[0], above), send(planes.at[0], halo.at[1], below)]
    fetches[2].wait()
    fetches[5].wait()
    bias2[me] = as_column(row2[...], OWN)
    mine, mine_bias = w2.at[core, y, me], bias2.at[me]
    cross_w = [send(mine, mine, mirror), send(mine_bias, mine_bias, mirror)]
    own_w = []
    for peer in x_peers:
        own_w += [send(mine, mine, peer), send(mine_bias, mine_bias, peer)]
    fill_pick(pick1, 3)
    planes[1] = raw[:, 1, :]
    planes[2] = raw[:, 2, :]
    fetches[4].wait()
    bias1[...] = as_column(row1[...], MID)
    fetches[1].wait()

    def place(i, part, plane):
        high, low_part = split(plane)
        at = slice(part * 256, (part + 1) * 256)
        rows1[i * CIN : (i + 1) * CIN, at] = high
        rows1[4 * CIN + i * CIN : 4 * CIN + (i + 1) * CIN, at] = low_part

    for i in range(4):
        for part in range(2):
            if 0 <= 2 * part + i - 1 < 4:
                place(i, part, planes[2 * part + i - 1])
    fetches[3].wait()
    high, low_part = split(w1[...])
    w1s[:MID] = high
    w1s[MID:] = low_part
    fill_pick(pick2, 2)
    wait(edges)
    place(0, 0, jnp.where(me > 0, halo[0], 0.0))
    place(3, 1, jnp.where(me < 7, halo[1], 0.0))
    columns(rows1, pick1, grid1, CIN)
    wait(cross_w)
    other, other_bias = w2.at[core, y, partner], bias2.at[partner]
    for peer in x_peers:
        own_w += [send(other, other, peer), send(other_bias, other_bias, peer)]
    pre1[...] = forward(w1s, grid1, pairs1, MID, CIN * 64) + bias1[...]
    hidden[me, :MID] = smooth(pre1[...])

    mine = hidden.at[me]
    cross = send(mine, mine, z_peer)
    own = [send(mine, mine, peer) for peer in x_peers]
    wait(own_w)
    mine = w2.at[core, y]
    spread_w = [send(mine, mine, peer) for peer in y_peers]
    fill_fold(fold)
    fill_spread(spread1, 3)
    cross.wait()
    other = hidden.at[partner]
    own += [send(other, other, peer) for peer in x_peers]
    wait(spread_w)
    half = w2.at[core]
    share = send(half, half, core_peer)

    def take_weights(part):
        for quarter in range(4):
            for s in range(8):
                high, low_part = split(w2[part, quarter, s])
                at = lanes(part * 2048 + quarter * 512, 512)
                w2s[s * OWN : (s + 1) * OWN, at] = high
                w2s[MID + s * OWN : MID + (s + 1) * OWN, at] = low_part

    take_weights(core)
    wait(own)

    lane = lax.broadcasted_iota(jnp.int32, (MID, 128), 1)
    first = lane < 64
    zero = jnp.zeros((MID, 128), F32)

    def put(i, m, value):
        high, low_part = split(value)
        at = slice(m * 128, (m + 1) * 128)
        rows2[i * MID : (i + 1) * MID, at] = high
        rows2[4 * MID + i * MID : 4 * MID + (i + 1) * MID, at] = low_part

    for m in range(4):
        near, next_one = hidden[2 * m, :MID], hidden[2 * m + 1, :MID]
        before = hidden[2 * m - 1, :MID] if m > 0 else zero
        after = hidden[2 * m + 2, :MID] if m < 3 else zero
        put(0, m, jnp.where(first, pltpu.roll(before, 64, 1), near))
        put(1, m, jnp.where(first, near, pltpu.roll(next_one, 64, 1)))
        put(2, m, jnp.where(first, pltpu.roll(near, 64, 1), next_one))
        put(3, m, jnp.where(first, next_one, pltpu.roll(after, 64, 1)))
    columns(rows2, pick2, grid2, MID)
    share.wait()
    take_weights(1 - core)
    total = forward(w2s, grid2, pairs2, MID, MID * 64)
    for s in range(8):
        block = slice(s * OWN, (s + 1) * OWN)
        value = total[block] + bias2[s]
        pre2[s] = value
        grad2[s] = hidden[s, MID:] * slope(value)
    all_grad2 = jnp.concatenate([grad2[s] for s in range(8)], axis=0)
    own_columns(w2s, all_grad2, me, grid2, MID * 64)
    grad1[...] = own_planes(grid2, fold, taps2) * slope(pre1[...])
    kernel_grad(grad1[rows(32, 1 - core), :], pairs1, gw1, 32, CIN * 64)
    copies = [send(gw1, c1, core_peer)]
    kernel_grad(grad1[rows(32, core), :], pairs1, gw1_own, 32, CIN * 64)

    ones = jnp.ones((8, 128), BF16)

    def sums(value):
        high, low_part = split(value)
        rest = (value - high.astype(F32) - low_part.astype(F32)).astype(BF16)
        return (dot(ones, high, (1, 1)) + dot(ones, low_part, (1, 1)) + dot(ones, rest, (1, 1))) * (
            1.0 / SAMPLES
        )

    own_grad2 = grad2[me]
    gbias[...] = jnp.zeros((8, 128), F32)
    gbias[:, :MID] = sums(grad1[...])
    gbias[:, MID : MID + OWN] = sums(own_grad2)
    copies.append(send(gbias, c3, core_peer))
    wait(copies)
    s1[...] = gw1_own[...] + c1[...]
    s3[...] = gbias[...] + c3[...]
    copies = []
    for at, ((i, j), peer) in enumerate(xy_peers.items()):
        piece = s1.at[rows(8, flip(x, i)), lanes(flip(y, j) * 512, 512)]
        copies.append(send(piece, xy1.at[at], peer))
    copies += [send(s3, x3.at[k], x_peers[k]) for k in range(3)]
    kernel_grad(own_grad2, pairs2, gw2, OWN, MID * 64)
    early = send(gw2.at[:, lanes((1 - core) * 2048, 2048)], c2, core_peer)
    early.wait()
    s2[...] = gw2[:, lanes(core * 2048, 2048)] + c2[...]
    for k in (1, 2, 3):
        piece = s2.at[:, lanes(flip(y, k) * 512, 512)]
        copies.append(send(piece, y2.at[k - 1], y_peers[k - 1]))
    column_grad(w1s, grad1[...], grid1, MID, CIN * 64)
    out[...] = smooth(pre2[me])
    wait(copies)
    shared = lax.broadcasted_iota(jnp.int32, (8, 128), 1) < MID
    here = lanes(y * 512, 512)
    total = s1[rows(8, x), here] + xy1[0]
    for at in range(1, 15):
        total = total + xy1[at]
    n1[...] = total
    n2[...] = (s2[:, here] + y2[0]) + (y2[1] + y2[2])
    m3[...] = jnp.where(shared, (s3[...] + x3[0]) + (x3[1] + x3[2]), s3[...])
    copies = []
    for k in (1, 2, 3):
        there = lanes(flip(step, k) * 128, 128)
        copies.append(send(n1.at[:, there], r1.at[k - 1], b_peers[k - 1]))
        copies.append(send(n2.at[:, there], r2.at[k - 1], b_peers[k - 1]))
        copies.append(send(m3, y3.at[k - 1], y_peers[k - 1]))
    def back(i, part):
        return drows1[i * CIN : (i + 1) * CIN, part * 256 : (part + 1) * 256]

    wait(copies)
    here = lanes(step * 128, 128)
    o1[...] = (n1[:, here] + r1[0]) + (r1[1] + r1[2])
    o2[...] = (n2[:, here] + r2[0]) + (r2[1] + r2[2])
    n3[...] = (m3[...] + y3[0]) + (y3[1] + y3[2])
    copies = []
    for k in (1, 2, 3):
        copies.append(send(o1, a1.at[k - 1], a_peers[k - 1]))
        copies.append(send(n3, r3.at[k - 1], b_peers[k - 1]))
    copies.append(send(o2, a2, a_peers[0]))
    rows_grad(grid1, spread1, taps1, drows1, CIN)
    edge_out[0] = back(0, 0)
    edge_out[1] = back(3, 1)
    edges = [send(edge_out.at[0], edge_in.at[1], below), send(edge_out.at[1], edge_in.at[0], above)]
    tvol[:, 1, :] = back(2, 0) + back(0, 1)
    tvol[:, 2, :] = back(3, 0) + back(1, 1)
    inner[0] = back(1, 0)
    inner[1] = back(2, 1)
    wait(copies)
    o3[...] = (n3[...] + r3[0]) + (r3[1] + r3[2])
    own_rows = rows(8, core * 4 + x)
    at1 = y * 512 + step * 128
    at2 = core * 2048 + at1
    tw1[own_rows, lanes(at1, 128)] = (o1[...] + a1[0]) + (a1[1] + a1[2])
    tw2[:, lanes(at2, 128)] = o2[...] + a2[...]
    copies = []
    for peer in b_peers:
        here1 = tw1.at[own_rows, lanes(at1, 128)]
        here2 = tw2.at[:, lanes(at2, 128)]
        copies += [send(here1, here1, peer), send(here2, here2, peer)]
    copies += [send(o3, a3.at[k], a_peers[k]) for k in range(3)]
    wait(copies)
    piece1 = tw1.at[own_rows, lanes(y * 512, 512)]
    piece2 = tw2.at[:, lanes(core * 2048 + y * 512, 512)]
    back1 = {at: send(piece1, piece1, peer) for at, peer in xy_peers.items()}
    back2 = [send(piece2, piece2, peer) for peer in y_peers]
    near = o3[...] + a3[0]
    tbias[...] = jnp.where(shared, near + (a3[1] + a3[2]), near)
    wait(back2)
    here2 = tw2.at[:, lanes(core * 2048, 2048)]
    last = [send(here2, here2, core_peer)]
    for i in range(4):
        for j in range(4):
            if i or j:
                back1[i, j].wait()
        here1 = tw1.at[rows(8, core * 4 + flip(x, i)), :]
        last.append(send(here1, here1, core_peer))
    wait(edges)
    tvol[:, 0, :] = inner[0] + jnp.where(me > 0, edge_in[0], 0.0)
    tvol[:, 3, :] = inner[1] + jnp.where(me < 7, edge_in[1], 0.0)
    wait(last)


def stepped(vol, cot, w1, b1, w2, b2):
    shape = jax.ShapeDtypeStruct

    def vmem(*size):
        return pltpu.VMEM(size, F32)

    def half(*size):
        return pltpu.VMEM(size, BF16)

    return pl.pallas_call(
        step_kernel,
        out_shape=(
            shape((OWN, 128), F32),
            shape((MID, CIN * 64), F32),
            shape((OWN, MID * 64), F32),
            shape((8, 128), F32),
            shape((CIN, 4, 256), F32),
        ),
        in_specs=[
            pl.BlockSpec(memory_space=pltpu.HBM),
            pl.BlockSpec(memory_space=pltpu.HBM),
            pl.BlockSpec(memory_space=pltpu.HBM),
            pl.BlockSpec(memory_space=pltpu.HBM),
            pl.BlockSpec(memory_space=pltpu.HBM),
            pl.BlockSpec(memory_space=pltpu.HBM),
        ],
        out_specs=[pl.BlockSpec(memory_space=pltpu.VMEM)] * 5,
        scratch_shapes=[
            vmem(CIN, 4, 256), vmem(4, CIN, 256), vmem(2, CIN, 256),
            vmem(8, MID + OWN, 128), vmem(MID, 128), vmem(8, OWN, 128), vmem(8, OWN, 128),
            vmem(MID, CIN * 64), vmem(2, 4, 8, OWN, 512), vmem(MID, 128), vmem(8, OWN, 128),
            vmem(1, MID), vmem(1, OWN),
            half(8, 512, 256), half(8, 512, 256), half(8, 256, 512), half(8, 128, 128),
            half(8 * CIN, 512), half(8 * MID, 512), half(8 * CIN, 256), half(8, 2 * MID, 128),
            vmem(4 * CIN, 512),
            vmem(CIN * 64, 128), vmem(MID * 64, 128), half(CIN * 64, 256), half(MID * 64, 256),
            half(2 * MID, CIN * 64), half(2 * MID, MID * 64),
            vmem(MID, 128), vmem(32, CIN * 64), vmem(32, CIN * 64), vmem(OWN, MID * 64), vmem(8, 128),
            vmem(2, CIN, 256), vmem(2, CIN, 256), vmem(2, CIN, 256),
            vmem(32, 2048), vmem(8, 2048), vmem(8, 128),
            vmem(32, 2048), vmem(8, 2048), vmem(8, 128),
            vmem(15, 8, 512), vmem(3, 8, 128), vmem(8, 128),
            vmem(3, 8, 512), vmem(3, 8, 128),
            vmem(8, 512), vmem(8, 512), vmem(8, 128),
            vmem(3, 8, 128), vmem(3, 8, 128), vmem(3, 8, 128),
            vmem(8, 128), vmem(8, 128), vmem(8, 128),
            vmem(3, 8, 128), vmem(8, 128), vmem(3, 8, 128),
            pltpu.SemaphoreType.DMA((6,)),
            pltpu.SemaphoreType.DMA((128,)),
            pltpu.SemaphoreType.DMA((128,)),
        ],
        compiler_params=pltpu.CompilerParams(
            collective_id=0, has_side_effects=True, vmem_limit_bytes=60 << 20
        ),
        name="stepped",
    )(vol, cot, w1, b1, w2, b2)


def finish_kernel(out, gw1, gw2, gbias, gvol, to_out, to_w1, to_w2, to_b1, to_b2, to_vol, done):
    copies = [
        pltpu.make_async_copy(source, target, done.at[at])
        for at, (source, target) in enumerate(
            [(gw1, to_w1), (gw2, to_w2), (gvol, to_vol), (out, to_out)]
        )
    ]
    for copy in copies:
        copy.start()
    to_b1[...] = gbias[0, :MID]
    to_b2[...] = gbias[0, MID : MID + OWN]
    for copy in copies:
        copy.wait()


def finished(out, gw1, gw2, gbias, gvol):
    shape = jax.ShapeDtypeStruct
    anywhere = pl.BlockSpec(memory_space=pltpu.HBM)
    vmem = pl.BlockSpec(memory_space=pltpu.VMEM)
    return pl.pallas_call(
        finish_kernel,
        out_shape=(
            shape((OWN, 128), F32),
            shape((MID, CIN * 64), F32),
            shape((OWN, MID * 64), F32),
            shape((MID,), F32),
            shape((OWN,), F32),
            shape((CIN, 4, 256), F32),
        ),
        in_specs=[vmem] * 5,
        out_specs=[anywhere, anywhere, anywhere, vmem, vmem, anywhere],
        scratch_shapes=[pltpu.SemaphoreType.DMA((4,))],
        name="finished",
    )(out, gw1, gw2, gbias, gvol)


def on_device(volume, cotangent, w_first, b_first, w_second, b_second):
    results = stepped(
        volume[0], cotangent[0], w_first, b_first[None], w_second, b_second[None]
    )
    out, gw1, gw2, gb1, gb2, gvol = finished(*results)
    return (out[None], gvol[None], gw1, gb1, gw2, gb2)


def solution(mesh):
    in_specs = (
        P("dp", None, "space", None),
        P("dp", "space", None),
        P(),
        P(),
        P("space", None),
        P("space"),
    )
    out_specs = (
        P("dp", "space", None),
        P("dp", None, "space", None),
        P(),
        P(),
        P("space", None),
        P("space"),
    )
    return jax.shard_map(
        on_device, mesh=mesh, in_specs=in_specs, out_specs=out_specs, check_vma=False
    )
```

```python
import functools

import jax
import jax.numpy as jnp
from jax import lax
from jax.experimental import pallas as pl
from jax.experimental.pallas import tpu as pltpu
from jax.sharding import PartitionSpec as P

MESH = pl.DeviceIdType.MESH
F32 = jnp.float32
BF16 = jnp.bfloat16
SLOPE = 0.3
CIN = 32
MID = 64
OWN = 8
SAMPLES = 64
UNROLL = 4


def split(value):
    high = value.astype(BF16)
    low = (value - high.astype(F32)).astype(BF16)
    return high, low


def dot(a, b, contract):
    return lax.dot_general(a, b, ((contract[:1], contract[1:]), ((), ())), preferred_element_type=F32)


def smooth(pre):
    decay = jnp.exp(-jnp.abs(pre))
    soft = jnp.maximum(pre, 0.0) + jnp.log(1.0 + decay)
    return SLOPE * pre + (1.0 - SLOPE) * soft


def slope(pre):
    decay = jnp.exp(-jnp.abs(pre))
    return SLOPE + (1.0 - SLOPE) * (jnp.where(pre >= 0.0, 1.0, decay) / (1.0 + decay))


def source_of(column, tap, log_half):
    half = 1 << log_half
    width = 2 * half
    slab = lax.shift_right_logical(column, 2 * log_half)
    row = lax.shift_right_logical(column, log_half) & (half - 1)
    cell = column & (half - 1)
    high = 2 * row + lax.shift_right_logical(tap, 2) - 1
    low = 2 * cell + (tap & 3) - 1
    inside = (high >= 0) & (high < width) & (low >= 0) & (low < width)
    return jnp.where(inside, slab * (width * width) + high * width + low, -1)


def fill_pick(pick, log_half):
    @pl.loop(0, 8)
    def _(pair):
        lane = lax.broadcasted_iota(jnp.int32, (8, 256), 1)
        source = source_of(lane & 127, 2 * pair + lax.shift_right_logical(lane, 7), log_half)
        cell = lax.broadcasted_iota(jnp.int32, (512, 256), 0)
        pick[pair] = jnp.where(cell == source[0:1], 1.0, 0.0).astype(BF16)


def fill_spread(spread, log_half):
    @pl.loop(0, 8)
    def _(pair):
        row = lax.broadcasted_iota(jnp.int32, (256, 128), 0)
        source = source_of(row & 127, 2 * pair + lax.shift_right_logical(row, 7), log_half)
        cell = lax.broadcasted_iota(jnp.int32, (256, 128), 1)
        for part in range(4):
            spread[pair, :, part * 128 : (part + 1) * 128] = jnp.where(
                cell + part * 128 == source, 1.0, 0.0
            ).astype(BF16)


def columns(rows, pick, grid, channels, taps):
    half = 2 * channels

    @pl.loop(0, 8, unroll=UNROLL)
    def _(pair):
        both = dot(rows[...], pick[pair], (1, 0))
        value = both[:half] + both[half:]
        for order, i in enumerate(taps):
            for second in range(2):
                grid[pl.ds(i * 16 + 2 * pair + second, channels, stride=64), :] = value[
                    order * channels : (order + 1) * channels, second * 128 : (second + 1) * 128
                ]


def all_columns(rows, pick, grid):
    lane = lax.broadcasted_iota(jnp.int32, (MID, 128), 1)

    @pl.loop(0, 8, unroll=UNROLL)
    def _(pair):
        both = dot(rows[...], pick[pair], (1, 0))
        value = both[: 2 * MID] + both[2 * MID :]
        for second in range(2):
            even = value[:MID, second * 128 : (second + 1) * 128]
            odd = value[MID:, second * 128 : (second + 1) * 128]
            at = 2 * pair + second
            before = jnp.where(lane < 16, 0.0, pltpu.roll(odd, 16, 1))
            after = jnp.where(lane >= 112, 0.0, pltpu.roll(even, 112, 1))
            grid[pl.ds(at, MID, stride=64), :] = before
            grid[pl.ds(16 + at, MID, stride=64), :] = even
            grid[pl.ds(32 + at, MID, stride=64), :] = odd
            grid[pl.ds(48 + at, MID, stride=64), :] = after


def forward(weights, grid, pair_grid, count, depth):
    chunk = 512

    def body(step, total):
        at = pl.multiple_of(step * chunk, chunk)
        high, low = split(grid[pl.ds(at, chunk), :])
        pair_grid[pl.ds(at, chunk), :128] = high
        pair_grid[pl.ds(at, chunk), 128:] = low
        return total + dot(weights[:, pl.ds(at, chunk)], pair_grid[pl.ds(at, chunk), :], (1, 0))

    total = lax.fori_loop(0, depth // chunk, body, jnp.zeros((2 * count, 256), F32), unroll=UNROLL)
    return (total[:count, :128] + total[:count, 128:]) + (total[count:, :128] + total[count:, 128:])


def kernel_grad(gradient, pair_grid, result, count, depth):
    chunk = 512
    high, low = split(gradient)
    both = jnp.concatenate(
        [jnp.concatenate([high, high], axis=1), jnp.concatenate([low, low], axis=1)], axis=0
    )

    @pl.loop(0, depth // chunk, unroll=UNROLL)
    def _(step):
        at = pl.multiple_of(step * chunk, chunk)
        value = dot(both, pair_grid[pl.ds(at, chunk), :], (1, 1))
        result[:, pl.ds(at, chunk)] = (value[:count] + value[count:]) * (1.0 / SAMPLES)


def column_grad(weights, gradient, grid, count, depth):
    chunk = 512
    high, low = split(gradient)
    both = jnp.concatenate(
        [jnp.concatenate([high, low], axis=1), jnp.concatenate([high, low], axis=1)], axis=0
    )

    @pl.loop(0, depth // chunk, unroll=UNROLL)
    def _(step):
        at = pl.multiple_of(step * chunk, chunk)
        value = dot(weights[:, pl.ds(at, chunk)], both, (0, 0))
        grid[pl.ds(at, chunk), :] = value[:, :128] + value[:, 128:]


def rows_grad(grid, spread, taps, total, channels):
    half = 4 * channels
    total[...] = jnp.zeros_like(total)

    @pl.loop(0, 8, unroll=UNROLL)
    def _(pair):
        for i in range(4):
            for second in range(2):
                high, low = split(grid[pl.ds(i * 16 + 2 * pair + second, channels, stride=64), :])
                lanes = slice(second * 128, (second + 1) * 128)
                taps[i * channels : (i + 1) * channels, lanes] = high
                taps[half + i * channels : half + (i + 1) * channels, lanes] = low
        both = dot(taps[...], spread[pair], (1, 0))
        total[...] += both[:half] + both[half:]


def fill_fold(fold):
    @pl.loop(0, 8)
    def _(pair):
        row = lax.broadcasted_iota(jnp.int32, (128, 128), 0)
        cell = source_of(row & 15, 2 * pair + lax.shift_right_logical(row, 6), 2)
        plane = lax.shift_right_logical(row, 5) & 1
        lane = lax.broadcasted_iota(jnp.int32, (128, 128), 1)
        fold[pair] = jnp.where((cell >= 0) & (lane == plane * 64 + cell), 1.0, 0.0).astype(BF16)


def own_columns(weights, gradient, me, grid, depth):
    chunk = 512
    lane = lax.broadcasted_iota(jnp.int32, (MID, 128), 1)
    near = pltpu.roll(gradient, (144 - 16 * me) % 128, 1)
    again = pltpu.roll(gradient, (176 - 16 * me) % 128, 1)
    chosen = jnp.where(lane < 48, near, again)
    outside = ((lane < 16) & (me == 0)) | ((lane >= 32) & (lane < 48) & (me == 7))
    high, low = split(jnp.where(outside, 0.0, chosen))
    packed = jnp.where(lane < 64, high.astype(F32), pltpu.roll(low.astype(F32), 64, 1)).astype(BF16)
    both = jnp.concatenate([packed, packed], axis=0)

    @pl.loop(0, depth // chunk, unroll=UNROLL)
    def _(step):
        at = pl.multiple_of(step * chunk, chunk)
        value = dot(weights[:, pl.ds(at, chunk)], both, (0, 0))
        grid[pl.ds(at, chunk), :] = value + pltpu.roll(value, 64, 1)


def own_planes(grid, fold, taps):
    lane = lax.broadcasted_iota(jnp.int32, (MID, 128), 1)
    slot = lax.shift_right_logical(lane, 4)

    def body(pair, total):
        value = jnp.zeros((MID, 128), F32)
        for second in range(2):
            for order, i in enumerate((3, 1, 0, 2)):
                part = grid[pl.ds(i * 16 + 2 * pair + second, MID, stride=64), :]
                value = jnp.where(slot == 4 * second + order, part, value)
        high, low = split(value)
        taps[pair, :MID] = high
        taps[pair, MID:] = low
        return total + dot(taps[pair], fold[pair], (1, 0))

    total = lax.fori_loop(0, 8, body, jnp.zeros((2 * MID, 128), F32), unroll=UNROLL)
    return total[:MID] + total[MID:]


def copy_to(source, target, sends, receives, at, device):
    return pltpu.make_async_remote_copy(
        src_ref=source,
        dst_ref=target,
        send_sem=sends.at[at],
        recv_sem=receives.at[at],
        device_id=device,
        device_id_type=MESH,
    )


def flip(index, k):
    if k == 0:
        return index
    if k == 1:
        return index + 1 - 2 * (index % 2)
    if k == 2:
        return (index + 2) % 4
    return 3 - index


def step_kernel(
    vol_in, cot_in, w1_in, b1_in, w2_in, b2_in,
    to_out, to_w1, to_w2, to_bias, to_vol,
    out, tw1, tw2, tbias, tvol,
    raw, planes, halo, hidden, pre1, pre2, grad2, w1, w2, bias1, bias2, row1, row2,
    pick1, pick2, spread1, fold,
    rows1, rows2, taps1, taps2, drows1,
    grid1, grid2, pairs1, pairs2, w1s, w2s,
    grad1, gw1, gw1_own, gw2, gbias, edge_out, edge_in, inner,
    c1, c2, c3, s1, s2, s3, xy1, x3, m3, y2, y3, n1, n2, n3,
    r1, r2, r3, o1, o2, o3, a1, a2, a3,
    loads, stores, sends, receives,
):
    dp, me = lax.axis_index("dp"), lax.axis_index("space")
    core, low, y = dp % 2, (dp // 2) % 8, dp // 16
    x, far = me // 2, me % 2
    run, step = 2 * far + low // 4, low % 4
    partner = 2 * x + 1 - far
    core_peer = {"dp": dp + 1 - 2 * core, "space": me}
    z_peer = {"dp": dp, "space": partner}
    mirror = {"dp": y * 16 + (7 - low) * 2 + core, "space": partner}
    x_peers = [{"dp": dp, "space": 2 * flip(x, k) + far} for k in (1, 2, 3)]
    y_peers = [{"dp": flip(y, k) * 16 + dp % 16, "space": me} for k in (1, 2, 3)]
    xy_peers = {
        (i, j): {"dp": flip(y, j) * 16 + dp % 16, "space": 2 * flip(x, i) + far}
        for i in range(4)
        for j in range(4)
        if i or j
    }
    b_peers = [
        {"dp": y * 16 + (4 * (low // 4) + flip(step, k)) * 2 + core, "space": me} for k in (1, 2, 3)
    ]
    a_peers = [
        {
            "dp": y * 16 + (4 * (flip(run, k) % 2) + step) * 2 + core,
            "space": 2 * x + flip(run, k) // 2,
        }
        for k in (1, 2, 3)
    ]
    space_peers = [{"dp": dp, "space": (me + k) % 8} for k in range(1, 8)]
    above, below = space_peers[0], space_peers[6]
    barrier = pltpu.get_barrier_semaphore()
    peers = [*space_peers, core_peer, mirror, *b_peers, *a_peers]
    peers += [peer for (_, j), peer in xy_peers.items() if j]
    for peer in peers:
        pl.semaphore_signal(barrier, inc=1, device_id=peer, device_id_type=MESH)

    used = [0]

    def send(source, target, peer):
        copy = copy_to(source, target, sends, receives, used[0], peer)
        used[0] += 1
        copy.start()
        return copy

    stored = []

    def store(source, target):
        copy = pltpu.make_async_copy(source, target, stores.at[len(stored)])
        stored.append(copy)
        copy.start()

    def wait(copies):
        for copy in copies:
            copy.wait()

    def rows(count, index):
        return pl.ds(pl.multiple_of(count * index, 8), count)

    def lanes(start, count):
        return pl.ds(pl.multiple_of(start, 128), count)

    fetches = [
        pltpu.make_async_copy(vol_in, raw, loads.at[0]),
        pltpu.make_async_copy(cot_in, hidden.at[me, MID:], loads.at[1]),
        pltpu.make_async_copy(
            w2_in.at[:, lanes(core * 2048 + y * 512, 512)], w2.at[core, y, me], loads.at[2]
        ),
        pltpu.make_async_copy(w1_in, w1, loads.at[3]),
        pltpu.make_async_copy(b1_in, row1, loads.at[4]),
        pltpu.make_async_copy(b2_in, row2, loads.at[5]),
    ]
    for fetch in fetches:
        fetch.start()

    def as_column(row, count):
        down = lax.broadcasted_iota(jnp.int32, (count, count), 0)
        along = lax.broadcasted_iota(jnp.int32, (count, count), 1)
        diagonal = jnp.where(down == along, jnp.broadcast_to(row, (count, count)), 0.0)
        return jnp.broadcast_to(jnp.sum(diagonal, axis=1, keepdims=True), (count, 128))

    fetches[0].wait()
    planes[0] = raw[:, 0, :]
    planes[3] = raw[:, 3, :]
    pl.semaphore_wait(barrier, len(peers))

    edges = [send(planes.at[3], halo.at[0], above), send(planes.at[0], halo.at[1], below)]
    fetches[2].wait()
    fetches[5].wait()
    bias2[me] = as_column(row2[...], OWN)
    mine, mine_bias = w2.at[core, y, me], bias2.at[me]
    cross_w = [send(mine, mine, mirror), send(mine_bias, mine_bias, mirror)]
    own_w = []
    for peer in x_peers:
        own_w += [send(mine, mine, peer), send(mine_bias, mine_bias, peer)]
    fill_pick(pick1, 3)
    planes[1] = raw[:, 1, :]
    planes[2] = raw[:, 2, :]
    fetches[4].wait()
    bias1[...] = as_column(row1[...], MID)
    fetches[1].wait()

    def place(i, part, plane):
        high, low_part = split(plane)
        at = slice(part * 256, (part + 1) * 256)
        group, order = (0, i - 1) if i in (1, 2) else (1, i // 3)
        rows1[group, order * CIN : (order + 1) * CIN, at] = high
        rows1[group, 2 * CIN + order * CIN : 2 * CIN + (order + 1) * CIN, at] = low_part

    for i in range(4):
        for part in range(2):
            if 0 <= 2 * part + i - 1 < 4:
                place(i, part, planes[2 * part + i - 1])
    fetches[3].wait()
    high, low_part = split(w1[...])
    w1s[:MID] = high
    w1s[MID:] = low_part
    columns(rows1.at[0], pick1, grid1, CIN, (1, 2))
    fill_pick(pick2, 2)
    wait(edges)
    place(0, 0, jnp.where(me > 0, halo[0], 0.0))
    place(3, 1, jnp.where(me < 7, halo[1], 0.0))
    columns(rows1.at[1], pick1, grid1, CIN, (0, 3))
    wait(cross_w)
    other, other_bias = w2.at[core, y, partner], bias2.at[partner]
    for peer in x_peers:
        own_w += [send(other, other, peer), send(other_bias, other_bias, peer)]
    pre1[...] = forward(w1s, grid1, pairs1, MID, CIN * 64) + bias1[...]
    hidden[me, :MID] = smooth(pre1[...])

    mine = hidden.at[me]
    cross = send(mine, mine, z_peer)
    own = [send(mine, mine, peer) for peer in x_peers]
    wait(own_w)
    mine = w2.at[core, y]
    spread_w = [send(mine, mine, peer) for peer in y_peers]
    fill_fold(fold)
    fill_spread(spread1, 3)
    cross.wait()
    other = hidden.at[partner]
    own += [send(other, other, peer) for peer in x_peers]
    wait(spread_w)
    half = w2.at[core]
    share = send(half, half, core_peer)

    def take_weights(part):
        for quarter in range(4):
            for s in range(8):
                high, low_part = split(w2[part, quarter, s])
                at = lanes(part * 2048 + quarter * 512, 512)
                w2s[s * OWN : (s + 1) * OWN, at] = high
                w2s[MID + s * OWN : MID + (s + 1) * OWN, at] = low_part

    take_weights(core)
    wait(own)

    first = lax.broadcasted_iota(jnp.int32, (MID, 128), 1) < 64

    def put(odd, m, value):
        high, low_part = split(value)
        at = slice(m * 128, (m + 1) * 128)
        rows2[odd * MID : (odd + 1) * MID, at] = high
        rows2[2 * MID + odd * MID : 2 * MID + (odd + 1) * MID, at] = low_part

    for m in range(4):
        near, next_one = hidden[2 * m, :MID], hidden[2 * m + 1, :MID]
        put(0, m, jnp.where(first, near, pltpu.roll(next_one, 64, 1)))
        put(1, m, jnp.where(first, pltpu.roll(near, 64, 1), next_one))
    all_columns(rows2, pick2, grid2)
    share.wait()
    take_weights(1 - core)
    total = forward(w2s, grid2, pairs2, MID, MID * 64)
    for s in range(8):
        block = slice(s * OWN, (s + 1) * OWN)
        value = total[block] + bias2[s]
        pre2[s] = value
        grad2[s] = hidden[s, MID:] * slope(value)
    all_grad2 = jnp.concatenate([grad2[s] for s in range(8)], axis=0)
    own_columns(w2s, all_grad2, me, grid2, MID * 64)
    grad1[...] = own_planes(grid2, fold, taps2) * slope(pre1[...])
    kernel_grad(grad1[rows(32, 1 - core), :], pairs1, gw1, 32, CIN * 64)
    copies = [send(gw1, c1, core_peer)]
    kernel_grad(grad1[rows(32, core), :], pairs1, gw1_own, 32, CIN * 64)

    ones = jnp.ones((8, 128), BF16)

    def sums(value):
        high, low_part = split(value)
        rest = (value - high.astype(F32) - low_part.astype(F32)).astype(BF16)
        return (dot(ones, high, (1, 1)) + dot(ones, low_part, (1, 1)) + dot(ones, rest, (1, 1))) * (
            1.0 / SAMPLES
        )

    own_grad2 = grad2[me]
    gbias[...] = jnp.zeros((8, 128), F32)
    gbias[:, :MID] = sums(grad1[...])
    gbias[:, MID : MID + OWN] = sums(own_grad2)
    copies.append(send(gbias, c3, core_peer))
    wait(copies)
    s1[...] = gw1_own[...] + c1[...]
    s3[...] = gbias[...] + c3[...]
    copies = []
    for at, ((i, j), peer) in enumerate(xy_peers.items()):
        piece = s1.at[rows(8, flip(x, i)), lanes(flip(y, j) * 512, 512)]
        copies.append(send(piece, xy1.at[at], peer))
    copies += [send(s3, x3.at[k], x_peers[k]) for k in range(3)]
    kernel_grad(own_grad2, pairs2, gw2, OWN, MID * 64)
    early = send(gw2.at[:, lanes((1 - core) * 2048, 2048)], c2, core_peer)
    early.wait()
    s2[...] = gw2[:, lanes(core * 2048, 2048)] + c2[...]
    for k in (1, 2, 3):
        piece = s2.at[:, lanes(flip(y, k) * 512, 512)]
        copies.append(send(piece, y2.at[k - 1], y_peers[k - 1]))
    column_grad(w1s, grad1[...], grid1, MID, CIN * 64)
    out[...] = smooth(pre2[me])
    store(out, to_out)
    wait(copies)
    shared = lax.broadcasted_iota(jnp.int32, (8, 128), 1) < MID
    here = lanes(y * 512, 512)
    total = s1[rows(8, x), here] + xy1[0]
    for at in range(1, 15):
        total = total + xy1[at]
    n1[...] = total
    n2[...] = (s2[:, here] + y2[0]) + (y2[1] + y2[2])
    m3[...] = jnp.where(shared, (s3[...] + x3[0]) + (x3[1] + x3[2]), s3[...])
    copies = []
    for k in (1, 2, 3):
        there = lanes(flip(step, k) * 128, 128)
        copies.append(send(n1.at[:, there], r1.at[k - 1], b_peers[k - 1]))
        copies.append(send(n2.at[:, there], r2.at[k - 1], b_peers[k - 1]))
        copies.append(send(m3, y3.at[k - 1], y_peers[k - 1]))
    def back(i, part):
        return drows1[i * CIN : (i + 1) * CIN, part * 256 : (part + 1) * 256]

    wait(copies)
    here = lanes(step * 128, 128)
    o1[...] = (n1[:, here] + r1[0]) + (r1[1] + r1[2])
    o2[...] = (n2[:, here] + r2[0]) + (r2[1] + r2[2])
    n3[...] = (m3[...] + y3[0]) + (y3[1] + y3[2])
    copies = []
    for k in (1, 2, 3):
        copies.append(send(o1, a1.at[k - 1], a_peers[k - 1]))
        copies.append(send(n3, r3.at[k - 1], b_peers[k - 1]))
    copies.append(send(o2, a2, a_peers[0]))
    rows_grad(grid1, spread1, taps1, drows1, CIN)
    edge_out[0] = back(0, 0)
    edge_out[1] = back(3, 1)
    edges = [send(edge_out.at[0], edge_in.at[1], below), send(edge_out.at[1], edge_in.at[0], above)]
    tvol[:, 1, :] = back(2, 0) + back(0, 1)
    tvol[:, 2, :] = back(3, 0) + back(1, 1)
    inner[0] = back(1, 0)
    inner[1] = back(2, 1)
    wait(copies)
    o3[...] = (n3[...] + r3[0]) + (r3[1] + r3[2])
    own_rows = rows(8, core * 4 + x)
    at1 = y * 512 + step * 128
    at2 = core * 2048 + at1
    tw1[own_rows, lanes(at1, 128)] = (o1[...] + a1[0]) + (a1[1] + a1[2])
    tw2[:, lanes(at2, 128)] = o2[...] + a2[...]
    copies = []
    for peer in b_peers:
        here1 = tw1.at[own_rows, lanes(at1, 128)]
        here2 = tw2.at[:, lanes(at2, 128)]
        copies += [send(here1, here1, peer), send(here2, here2, peer)]
    copies += [send(o3, a3.at[k], a_peers[k]) for k in range(3)]
    wait(copies)
    piece1 = tw1.at[own_rows, lanes(y * 512, 512)]
    piece2 = tw2.at[:, lanes(core * 2048 + y * 512, 512)]
    back1 = {at: send(piece1, piece1, peer) for at, peer in xy_peers.items()}
    back2 = [send(piece2, piece2, peer) for peer in y_peers]
    near = o3[...] + a3[0]
    tbias[...] = jnp.where(shared, near + (a3[1] + a3[2]), near)
    store(tbias, to_bias)
    wait(back2)
    here2 = tw2.at[:, lanes(core * 2048, 2048)]
    last2 = send(here2, here2, core_peer)
    store(here2, to_w2.at[:, lanes(core * 2048, 2048)])
    last = []
    for i in range(4):
        for j in range(4):
            if i or j:
                back1[i, j].wait()
        block = rows(8, core * 4 + flip(x, i))
        last.append(send(tw1.at[block, :], tw1.at[block, :], core_peer))
        store(tw1.at[block, :], to_w1.at[block, :])
    wait(edges)
    tvol[:, 0, :] = inner[0] + jnp.where(me > 0, edge_in[0], 0.0)
    tvol[:, 3, :] = inner[1] + jnp.where(me < 7, edge_in[1], 0.0)
    store(tvol, to_vol)
    last2.wait()
    there = lanes((1 - core) * 2048, 2048)
    store(tw2.at[:, there], to_w2.at[:, there])
    for i in range(4):
        last[i].wait()
        block = rows(8, (1 - core) * 4 + flip(x, i))
        store(tw1.at[block, :], to_w1.at[block, :])
    wait(stored)


def stepped(vol, cot, w1, b1, w2, b2):
    shape = jax.ShapeDtypeStruct

    def vmem(*size):
        return pltpu.VMEM(size, F32)

    def half(*size):
        return pltpu.VMEM(size, BF16)

    return pl.pallas_call(
        step_kernel,
        out_shape=(
            shape((OWN, 128), F32),
            shape((MID, CIN * 64), F32),
            shape((OWN, MID * 64), F32),
            shape((8, 128), F32),
            shape((CIN, 4, 256), F32),
        ),
        in_specs=[
            pl.BlockSpec(memory_space=pltpu.HBM),
            pl.BlockSpec(memory_space=pltpu.HBM),
            pl.BlockSpec(memory_space=pltpu.HBM),
            pl.BlockSpec(memory_space=pltpu.HBM),
            pl.BlockSpec(memory_space=pltpu.HBM),
            pl.BlockSpec(memory_space=pltpu.HBM),
        ],
        out_specs=[pl.BlockSpec(memory_space=pltpu.HBM)] * 5,
        scratch_shapes=[
            vmem(OWN, 128), vmem(MID, CIN * 64), vmem(OWN, MID * 64), vmem(8, 128), vmem(CIN, 4, 256),
            vmem(CIN, 4, 256), vmem(4, CIN, 256), vmem(2, CIN, 256),
            vmem(8, MID + OWN, 128), vmem(MID, 128), vmem(8, OWN, 128), vmem(8, OWN, 128),
            vmem(MID, CIN * 64), vmem(2, 4, 8, OWN, 512), vmem(MID, 128), vmem(8, OWN, 128),
            vmem(1, MID), vmem(1, OWN),
            half(8, 512, 256), half(8, 512, 256), half(8, 256, 512), half(8, 128, 128),
            half(2, 4 * CIN, 512), half(4 * MID, 512), half(8 * CIN, 256), half(8, 2 * MID, 128),
            vmem(4 * CIN, 512),
            vmem(CIN * 64, 128), vmem(MID * 64, 128), half(CIN * 64, 256), half(MID * 64, 256),
            half(2 * MID, CIN * 64), half(2 * MID, MID * 64),
            vmem(MID, 128), vmem(32, CIN * 64), vmem(32, CIN * 64), vmem(OWN, MID * 64), vmem(8, 128),
            vmem(2, CIN, 256), vmem(2, CIN, 256), vmem(2, CIN, 256),
            vmem(32, 2048), vmem(8, 2048), vmem(8, 128),
            vmem(32, 2048), vmem(8, 2048), vmem(8, 128),
            vmem(15, 8, 512), vmem(3, 8, 128), vmem(8, 128),
            vmem(3, 8, 512), vmem(3, 8, 128),
            vmem(8, 512), vmem(8, 512), vmem(8, 128),
            vmem(3, 8, 128), vmem(3, 8, 128), vmem(3, 8, 128),
            vmem(8, 128), vmem(8, 128), vmem(8, 128),
            vmem(3, 8, 128), vmem(8, 128), vmem(3, 8, 128),
            pltpu.SemaphoreType.DMA((6,)),
            pltpu.SemaphoreType.DMA((16,)),
            pltpu.SemaphoreType.DMA((128,)),
            pltpu.SemaphoreType.DMA((128,)),
        ],
        compiler_params=pltpu.CompilerParams(
            collective_id=0, has_side_effects=True, vmem_limit_bytes=60 << 20
        ),
        name="stepped",
    )(vol, cot, w1, b1, w2, b2)


def finish_kernel(
    out, gw1, gw2, gbias, gvol, to_out, to_w1, to_w2, to_b1, to_b2, to_vol,
    out_here, w1_here, w2_here, bias_here, vol_here, done,
):
    through = [
        (gbias, bias_here, None),
        (gw1, w1_here, to_w1),
        (gw2, w2_here, to_w2),
        (gvol, vol_here, to_vol),
        (out, out_here, to_out),
    ]
    taken = [
        pltpu.make_async_copy(source, here, done.at[at])
        for at, (source, here, _) in enumerate(through)
    ]
    for copy in taken:
        copy.start()
    given = []
    for at, (_, here, target) in enumerate(through):
        taken[at].wait()
        if target is None:
            to_b1[...] = here[0, :MID]
            to_b2[...] = here[0, MID : MID + OWN]
        else:
            given.append(pltpu.make_async_copy(here, target, done.at[5 + at]))
            given[-1].start()
    for copy in given:
        copy.wait()


def finished(out, gw1, gw2, gbias, gvol):
    shape = jax.ShapeDtypeStruct
    anywhere = pl.BlockSpec(memory_space=pltpu.HBM)
    vmem = pl.BlockSpec(memory_space=pltpu.VMEM)
    return pl.pallas_call(
        finish_kernel,
        out_shape=(
            shape((OWN, 128), F32),
            shape((MID, CIN * 64), F32),
            shape((OWN, MID * 64), F32),
            shape((MID,), F32),
            shape((OWN,), F32),
            shape((CIN, 4, 256), F32),
        ),
        in_specs=[anywhere] * 5,
        out_specs=[anywhere, anywhere, anywhere, vmem, vmem, anywhere],
        scratch_shapes=[
            pltpu.VMEM((OWN, 128), F32),
            pltpu.VMEM((MID, CIN * 64), F32),
            pltpu.VMEM((OWN, MID * 64), F32),
            pltpu.VMEM((8, 128), F32),
            pltpu.VMEM((CIN, 4, 256), F32),
            pltpu.SemaphoreType.DMA((10,)),
        ],
        compiler_params=pltpu.CompilerParams(vmem_limit_bytes=60 << 20),
        name="finished",
    )(out, gw1, gw2, gbias, gvol)


def on_device(volume, cotangent, w_first, b_first, w_second, b_second):
    results = stepped(
        volume[0], cotangent[0], w_first, b_first[None], w_second, b_second[None]
    )
    out, gw1, gw2, gb1, gb2, gvol = finished(*results)
    return (out[None], gvol[None], gw1, gb1, gw2, gb2)


def solution(mesh):
    in_specs = (
        P("dp", None, "space", None),
        P("dp", "space", None),
        P(),
        P(),
        P("space", None),
        P("space"),
    )
    out_specs = (
        P("dp", "space", None),
        P("dp", None, "space", None),
        P(),
        P(),
        P("space", None),
        P("space"),
    )
    return jax.shard_map(
        on_device, mesh=mesh, in_specs=in_specs, out_specs=out_specs, check_vma=False
    )
```

```python
import functools

import jax
import jax.numpy as jnp
from jax import lax
from jax.experimental import pallas as pl
from jax.experimental.pallas import tpu as pltpu
from jax.sharding import PartitionSpec as P

MESH = pl.DeviceIdType.MESH
F32 = jnp.float32
BF16 = jnp.bfloat16
SLOPE = 0.3
CIN = 32
MID = 64
OWN = 8
SAMPLES = 64
UNROLL = 4


def split(value):
    high = value.astype(BF16)
    low = (value - high.astype(F32)).astype(BF16)
    return high, low


def dot(a, b, contract):
    return lax.dot_general(a, b, ((contract[:1], contract[1:]), ((), ())), preferred_element_type=F32)


def smooth(pre):
    decay = jnp.exp(-jnp.abs(pre))
    soft = jnp.maximum(pre, 0.0) + jnp.log(1.0 + decay)
    return SLOPE * pre + (1.0 - SLOPE) * soft


def slope(pre):
    decay = jnp.exp(-jnp.abs(pre))
    return SLOPE + (1.0 - SLOPE) * (jnp.where(pre >= 0.0, 1.0, decay) / (1.0 + decay))


def source_of(column, tap, log_half):
    half = 1 << log_half
    width = 2 * half
    slab = lax.shift_right_logical(column, 2 * log_half)
    row = lax.shift_right_logical(column, log_half) & (half - 1)
    cell = column & (half - 1)
    high = 2 * row + lax.shift_right_logical(tap, 2) - 1
    low = 2 * cell + (tap & 3) - 1
    inside = (high >= 0) & (high < width) & (low >= 0) & (low < width)
    return jnp.where(inside, slab * (width * width) + high * width + low, -1)


def fill_pick(pick, log_half):
    @pl.loop(0, 8)
    def _(pair):
        lane = lax.broadcasted_iota(jnp.int32, (8, 256), 1)
        source = source_of(lane & 127, 2 * pair + lax.shift_right_logical(lane, 7), log_half)
        cell = lax.broadcasted_iota(jnp.int32, (512, 256), 0)
        pick[pair] = jnp.where(cell == source[0:1], 1.0, 0.0).astype(BF16)


def fill_spread(spread, log_half):
    @pl.loop(0, 8)
    def _(pair):
        row = lax.broadcasted_iota(jnp.int32, (256, 128), 0)
        source = source_of(row & 127, 2 * pair + lax.shift_right_logical(row, 7), log_half)
        cell = lax.broadcasted_iota(jnp.int32, (256, 128), 1)
        for part in range(4):
            spread[pair, :, part * 128 : (part + 1) * 128] = jnp.where(
                cell + part * 128 == source, 1.0, 0.0
            ).astype(BF16)


def columns(rows, pick, grid, channels, taps):
    half = 2 * channels

    @pl.loop(0, 8, unroll=UNROLL)
    def _(pair):
        both = dot(rows[...], pick[pair], (1, 0))
        value = both[:half] + both[half:]
        for order, i in enumerate(taps):
            for second in range(2):
                grid[pl.ds(i * 16 + 2 * pair + second, channels, stride=64), :] = value[
                    order * channels : (order + 1) * channels, second * 128 : (second + 1) * 128
                ]


def all_columns(rows, pick, grid):
    lane = lax.broadcasted_iota(jnp.int32, (MID, 128), 1)

    @pl.loop(0, 8, unroll=UNROLL)
    def _(pair):
        both = dot(rows[...], pick[pair], (1, 0))
        value = both[: 2 * MID] + both[2 * MID :]
        for second in range(2):
            even = value[:MID, second * 128 : (second + 1) * 128]
            odd = value[MID:, second * 128 : (second + 1) * 128]
            at = 2 * pair + second
            before = jnp.where(lane < 16, 0.0, pltpu.roll(odd, 16, 1))
            after = jnp.where(lane >= 112, 0.0, pltpu.roll(even, 112, 1))
            grid[pl.ds(at, MID, stride=64), :] = before
            grid[pl.ds(16 + at, MID, stride=64), :] = even
            grid[pl.ds(32 + at, MID, stride=64), :] = odd
            grid[pl.ds(48 + at, MID, stride=64), :] = after


def forward(weights, grid, pair_grid, count, depth):
    chunk = 512

    def body(step, total):
        at = pl.multiple_of(step * chunk, chunk)
        high, low = split(grid[pl.ds(at, chunk), :])
        pair_grid[pl.ds(at, chunk), :128] = high
        pair_grid[pl.ds(at, chunk), 128:] = low
        return total + dot(weights[:, pl.ds(at, chunk)], pair_grid[pl.ds(at, chunk), :], (1, 0))

    total = lax.fori_loop(0, depth // chunk, body, jnp.zeros((2 * count, 256), F32), unroll=UNROLL)
    return (total[:count, :128] + total[:count, 128:]) + (total[count:, :128] + total[count:, 128:])


def kernel_grad(gradient, pair_grid, result, count, depth):
    chunk = 512
    high, low = split(gradient)
    both = jnp.concatenate(
        [jnp.concatenate([high, high], axis=1), jnp.concatenate([low, low], axis=1)], axis=0
    )

    @pl.loop(0, depth // chunk, unroll=UNROLL)
    def _(step):
        at = pl.multiple_of(step * chunk, chunk)
        value = dot(both, pair_grid[pl.ds(at, chunk), :], (1, 1))
        result[:, pl.ds(at, chunk)] = (value[:count] + value[count:]) * (1.0 / SAMPLES)


def column_grad(weights, gradient, grid, count, depth):
    chunk = 512
    high, low = split(gradient)
    both = jnp.concatenate(
        [jnp.concatenate([high, low], axis=1), jnp.concatenate([high, low], axis=1)], axis=0
    )

    @pl.loop(0, depth // chunk, unroll=UNROLL)
    def _(step):
        at = pl.multiple_of(step * chunk, chunk)
        value = dot(weights[:, pl.ds(at, chunk)], both, (0, 0))
        grid[pl.ds(at, chunk), :] = value[:, :128] + value[:, 128:]


def rows_grad(grid, spread, taps, total, channels):
    half = 4 * channels
    total[...] = jnp.zeros_like(total)

    @pl.loop(0, 8, unroll=UNROLL)
    def _(pair):
        for i in range(4):
            for second in range(2):
                high, low = split(grid[pl.ds(i * 16 + 2 * pair + second, channels, stride=64), :])
                lanes = slice(second * 128, (second + 1) * 128)
                taps[i * channels : (i + 1) * channels, lanes] = high
                taps[half + i * channels : half + (i + 1) * channels, lanes] = low
        both = dot(taps[...], spread[pair], (1, 0))
        total[...] += both[:half] + both[half:]


def fill_fold(fold):
    @pl.loop(0, 8)
    def _(pair):
        row = lax.broadcasted_iota(jnp.int32, (128, 128), 0)
        cell = source_of(row & 15, 2 * pair + lax.shift_right_logical(row, 6), 2)
        plane = lax.shift_right_logical(row, 5) & 1
        lane = lax.broadcasted_iota(jnp.int32, (128, 128), 1)
        fold[pair] = jnp.where((cell >= 0) & (lane == plane * 64 + cell), 1.0, 0.0).astype(BF16)


def own_columns(weights, gradient, me, grid, depth):
    chunk = 512
    lane = lax.broadcasted_iota(jnp.int32, (MID, 128), 1)
    near = pltpu.roll(gradient, (144 - 16 * me) % 128, 1)
    again = pltpu.roll(gradient, (176 - 16 * me) % 128, 1)
    chosen = jnp.where(lane < 48, near, again)
    outside = ((lane < 16) & (me == 0)) | ((lane >= 32) & (lane < 48) & (me == 7))
    high, low = split(jnp.where(outside, 0.0, chosen))
    packed = jnp.where(lane < 64, high.astype(F32), pltpu.roll(low.astype(F32), 64, 1)).astype(BF16)
    both = jnp.concatenate([packed, packed], axis=0)

    @pl.loop(0, depth // chunk, unroll=UNROLL)
    def _(step):
        at = pl.multiple_of(step * chunk, chunk)
        value = dot(weights[:, pl.ds(at, chunk)], both, (0, 0))
        grid[pl.ds(at, chunk), :] = value + pltpu.roll(value, 64, 1)


def own_planes(grid, fold, taps):
    lane = lax.broadcasted_iota(jnp.int32, (MID, 128), 1)
    slot = lax.shift_right_logical(lane, 4)

    def body(pair, total):
        value = jnp.zeros((MID, 128), F32)
        for second in range(2):
            for order, i in enumerate((3, 1, 0, 2)):
                part = grid[pl.ds(i * 16 + 2 * pair + second, MID, stride=64), :]
                value = jnp.where(slot == 4 * second + order, part, value)
        high, low = split(value)
        taps[pair, :MID] = high
        taps[pair, MID:] = low
        return total + dot(taps[pair], fold[pair], (1, 0))

    total = lax.fori_loop(0, 8, body, jnp.zeros((2 * MID, 128), F32), unroll=UNROLL)
    return total[:MID] + total[MID:]


def copy_to(source, target, sends, receives, at, device):
    return pltpu.make_async_remote_copy(
        src_ref=source,
        dst_ref=target,
        send_sem=sends.at[at],
        recv_sem=receives.at[at],
        device_id=device,
        device_id_type=MESH,
    )


def flip(index, k):
    if k == 0:
        return index
    if k == 1:
        return index + 1 - 2 * (index % 2)
    if k == 2:
        return (index + 2) % 4
    return 3 - index


def step_kernel(
    vol_in, cot_in, w1_in, b1_in, w2_in, b2_in,
    to_out, to_w1, to_w2, to_bias, to_vol,
    out, tw1, tw2, tbias, tvol,
    raw, planes, halo, hidden, pre1, pre2, grad2, w1, w2, bias1, bias2, row1, row2,
    pick1, pick2, spread1, fold,
    rows1, rows2, taps1, taps2, drows1,
    grid1, grid2, pairs1, pairs2, w1s, w2s,
    grad1, gw1, gw1_own, gw2, gbias, edge_out, edge_in, inner,
    c1, c2, c3, s1, s2, s3, xy1, x3, m3, y2, y3, n1, n2, n3,
    r1, r2, r3, o1, o2, o3, a1, a2, a3,
    loads, stores, sends, receives,
):
    dp, me = lax.axis_index("dp"), lax.axis_index("space")
    core, low, y = dp % 2, (dp // 2) % 8, dp // 16
    x, far = me // 2, me % 2
    run, step = 2 * far + low // 4, low % 4
    partner = 2 * x + 1 - far
    core_peer = {"dp": dp + 1 - 2 * core, "space": me}
    z_peer = {"dp": dp, "space": partner}
    mirror = {"dp": y * 16 + (7 - low) * 2 + core, "space": partner}
    x_peers = [{"dp": dp, "space": 2 * flip(x, k) + far} for k in (1, 2, 3)]
    y_peers = [{"dp": flip(y, k) * 16 + dp % 16, "space": me} for k in (1, 2, 3)]
    xy_peers = {
        (i, j): {"dp": flip(y, j) * 16 + dp % 16, "space": 2 * flip(x, i) + far}
        for i in range(4)
        for j in range(4)
        if i or j
    }
    b_peers = [
        {"dp": y * 16 + (4 * (low // 4) + flip(step, k)) * 2 + core, "space": me} for k in (1, 2, 3)
    ]
    a_peers = [
        {
            "dp": y * 16 + (4 * (flip(run, k) % 2) + step) * 2 + core,
            "space": 2 * x + flip(run, k) // 2,
        }
        for k in (1, 2, 3)
    ]
    space_peers = [{"dp": dp, "space": (me + k) % 8} for k in range(1, 8)]
    above, below = space_peers[0], space_peers[6]
    barrier = pltpu.get_barrier_semaphore()
    peers = [*space_peers, core_peer, mirror, *b_peers, *a_peers]
    peers += [peer for (_, j), peer in xy_peers.items() if j]
    for peer in peers:
        pl.semaphore_signal(barrier, inc=1, device_id=peer, device_id_type=MESH)

    used = [0]

    def send(source, target, peer):
        copy = copy_to(source, target, sends, receives, used[0], peer)
        used[0] += 1
        copy.start()
        return copy

    stored = []

    def store(source, target):
        copy = pltpu.make_async_copy(source, target, stores.at[len(stored)])
        stored.append(copy)
        copy.start()

    def wait(copies):
        for copy in copies:
            copy.wait()

    def rows(count, index):
        return pl.ds(pl.multiple_of(count * index, 8), count)

    def lanes(start, count):
        return pl.ds(pl.multiple_of(start, 128), count)

    fetches = [
        pltpu.make_async_copy(vol_in, raw, loads.at[0]),
        pltpu.make_async_copy(cot_in, hidden.at[me, MID:], loads.at[1]),
        pltpu.make_async_copy(
            w2_in.at[:, lanes(core * 2048 + y * 512, 512)], w2.at[core, y, me], loads.at[2]
        ),
        pltpu.make_async_copy(w1_in, w1, loads.at[3]),
        pltpu.make_async_copy(b1_in, row1, loads.at[4]),
        pltpu.make_async_copy(b2_in, row2, loads.at[5]),
    ]
    for fetch in fetches:
        fetch.start()

    def as_column(row, count):
        down = lax.broadcasted_iota(jnp.int32, (count, count), 0)
        along = lax.broadcasted_iota(jnp.int32, (count, count), 1)
        diagonal = jnp.where(down == along, jnp.broadcast_to(row, (count, count)), 0.0)
        return jnp.broadcast_to(jnp.sum(diagonal, axis=1, keepdims=True), (count, 128))

    fetches[0].wait()
    planes[0] = raw[:, 0, :]
    planes[3] = raw[:, 3, :]
    pl.semaphore_wait(barrier, len(peers))

    edges = [send(planes.at[3], halo.at[0], above), send(planes.at[0], halo.at[1], below)]
    fetches[2].wait()
    fetches[5].wait()
    bias2[me] = as_column(row2[...], OWN)
    mine, mine_bias = w2.at[core, y, me], bias2.at[me]
    cross_w = [send(mine, mine, mirror), send(mine_bias, mine_bias, mirror)]
    own_w = []
    for peer in x_peers:
        own_w += [send(mine, mine, peer), send(mine_bias, mine_bias, peer)]
    fill_pick(pick1, 3)
    planes[1] = raw[:, 1, :]
    planes[2] = raw[:, 2, :]
    fetches[4].wait()
    bias1[...] = as_column(row1[...], MID)
    fetches[1].wait()

    def place(i, part, plane):
        high, low_part = split(plane)
        at = slice(part * 256, (part + 1) * 256)
        group, order = (0, i - 1) if i in (1, 2) else (1, i // 3)
        rows1[group, order * CIN : (order + 1) * CIN, at] = high
        rows1[group, 2 * CIN + order * CIN : 2 * CIN + (order + 1) * CIN, at] = low_part

    for i in range(4):
        for part in range(2):
            if 0 <= 2 * part + i - 1 < 4:
                place(i, part, planes[2 * part + i - 1])
    fetches[3].wait()
    high, low_part = split(w1[...])
    w1s[:MID] = high
    w1s[MID:] = low_part
    columns(rows1.at[0], pick1, grid1, CIN, (1, 2))
    fill_pick(pick2, 2)
    wait(edges)
    place(0, 0, jnp.where(me > 0, halo[0], 0.0))
    place(3, 1, jnp.where(me < 7, halo[1], 0.0))
    columns(rows1.at[1], pick1, grid1, CIN, (0, 3))
    wait(cross_w)
    other, other_bias = w2.at[core, y, partner], bias2.at[partner]
    for peer in x_peers:
        own_w += [send(other, other, peer), send(other_bias, other_bias, peer)]
    pre1[...] = forward(w1s, grid1, pairs1, MID, CIN * 64) + bias1[...]
    hidden[me, :MID] = smooth(pre1[...])

    mine = hidden.at[me]
    cross = send(mine, mine, z_peer)
    own = [send(mine, mine, peer) for peer in x_peers]
    wait(own_w)
    mine = w2.at[core, y]
    spread_w = [send(mine, mine, peer) for peer in y_peers]
    fill_fold(fold)
    fill_spread(spread1, 3)
    cross.wait()
    other = hidden.at[partner]
    own += [send(other, other, peer) for peer in x_peers]
    wait(spread_w)
    half = w2.at[core]
    share = send(half, half, core_peer)

    def take_weights(part):
        for quarter in range(4):
            for s in range(8):
                high, low_part = split(w2[part, quarter, s])
                at = lanes(part * 2048 + quarter * 512, 512)
                w2s[s * OWN : (s + 1) * OWN, at] = high
                w2s[MID + s * OWN : MID + (s + 1) * OWN, at] = low_part

    take_weights(core)
    wait(own)

    first = lax.broadcasted_iota(jnp.int32, (MID, 128), 1) < 64

    def put(odd, m, value):
        high, low_part = split(value)
        at = slice(m * 128, (m + 1) * 128)
        rows2[odd * MID : (odd + 1) * MID, at] = high
        rows2[2 * MID + odd * MID : 2 * MID + (odd + 1) * MID, at] = low_part

    for m in range(4):
        near, next_one = hidden[2 * m, :MID], hidden[2 * m + 1, :MID]
        put(0, m, jnp.where(first, near, pltpu.roll(next_one, 64, 1)))
        put(1, m, jnp.where(first, pltpu.roll(near, 64, 1), next_one))
    all_columns(rows2, pick2, grid2)
    share.wait()
    take_weights(1 - core)
    total = forward(w2s, grid2, pairs2, MID, MID * 64)
    for s in range(8):
        block = slice(s * OWN, (s + 1) * OWN)
        value = total[block] + bias2[s]
        pre2[s] = value
        grad2[s] = hidden[s, MID:] * slope(value)
    all_grad2 = jnp.concatenate([grad2[s] for s in range(8)], axis=0)
    own_columns(w2s, all_grad2, me, grid2, MID * 64)
    grad1[...] = own_planes(grid2, fold, taps2) * slope(pre1[...])
    kernel_grad(grad1[rows(32, 1 - core), :], pairs1, gw1, 32, CIN * 64)
    copies = [send(gw1, c1, core_peer)]
    kernel_grad(grad1[rows(32, core), :], pairs1, gw1_own, 32, CIN * 64)

    ones = jnp.ones((8, 128), BF16)

    def sums(value):
        high, low_part = split(value)
        rest = (value - high.astype(F32) - low_part.astype(F32)).astype(BF16)
        return (dot(ones, high, (1, 1)) + dot(ones, low_part, (1, 1)) + dot(ones, rest, (1, 1))) * (
            1.0 / SAMPLES
        )

    own_grad2 = grad2[me]
    gbias[...] = jnp.zeros((8, 128), F32)
    gbias[:, :MID] = sums(grad1[...])
    gbias[:, MID : MID + OWN] = sums(own_grad2)
    copies.append(send(gbias, c3, core_peer))
    wait(copies)
    s1[...] = gw1_own[...] + c1[...]
    s3[...] = gbias[...] + c3[...]
    copies = []
    for at, ((i, j), peer) in enumerate(xy_peers.items()):
        piece = s1.at[rows(8, flip(x, i)), lanes(flip(y, j) * 512, 512)]
        copies.append(send(piece, xy1.at[at], peer))
    copies += [send(s3, x3.at[k], x_peers[k]) for k in range(3)]
    kernel_grad(own_grad2, pairs2, gw2, OWN, MID * 64)
    early = send(gw2.at[:, lanes((1 - core) * 2048, 2048)], c2, core_peer)
    early.wait()
    s2[...] = gw2[:, lanes(core * 2048, 2048)] + c2[...]
    for k in (1, 2, 3):
        piece = s2.at[:, lanes(flip(y, k) * 512, 512)]
        copies.append(send(piece, y2.at[k - 1], y_peers[k - 1]))
    column_grad(w1s, grad1[...], grid1, MID, CIN * 64)
    out[...] = smooth(pre2[me])
    store(out, to_out)
    wait(copies)
    shared = lax.broadcasted_iota(jnp.int32, (8, 128), 1) < MID
    here = lanes(y * 512, 512)
    total = s1[rows(8, x), here] + xy1[0]
    for at in range(1, 15):
        total = total + xy1[at]
    n1[...] = total
    n2[...] = (s2[:, here] + y2[0]) + (y2[1] + y2[2])
    m3[...] = jnp.where(shared, (s3[...] + x3[0]) + (x3[1] + x3[2]), s3[...])
    copies = []
    for k in (1, 2, 3):
        there = lanes(flip(step, k) * 128, 128)
        copies.append(send(n1.at[:, there], r1.at[k - 1], b_peers[k - 1]))
        copies.append(send(n2.at[:, there], r2.at[k - 1], b_peers[k - 1]))
        copies.append(send(m3, y3.at[k - 1], y_peers[k - 1]))
    def back(i, part):
        return drows1[i * CIN : (i + 1) * CIN, part * 256 : (part + 1) * 256]

    wait(copies)
    here = lanes(step * 128, 128)
    o1[...] = (n1[:, here] + r1[0]) + (r1[1] + r1[2])
    o2[...] = (n2[:, here] + r2[0]) + (r2[1] + r2[2])
    n3[...] = (m3[...] + y3[0]) + (y3[1] + y3[2])
    copies = []
    for k in (1, 2, 3):
        copies.append(send(o1, a1.at[k - 1], a_peers[k - 1]))
        copies.append(send(n3, r3.at[k - 1], b_peers[k - 1]))
    copies.append(send(o2, a2, a_peers[0]))
    rows_grad(grid1, spread1, taps1, drows1, CIN)
    edge_out[0] = back(0, 0)
    edge_out[1] = back(3, 1)
    edges = [send(edge_out.at[0], edge_in.at[1], below), send(edge_out.at[1], edge_in.at[0], above)]
    tvol[:, 1, :] = back(2, 0) + back(0, 1)
    tvol[:, 2, :] = back(3, 0) + back(1, 1)
    inner[0] = back(1, 0)
    inner[1] = back(2, 1)
    wait(copies)
    o3[...] = (n3[...] + r3[0]) + (r3[1] + r3[2])
    own_rows = rows(8, core * 4 + x)
    at1 = y * 512 + step * 128
    at2 = core * 2048 + at1
    tw1[own_rows, lanes(at1, 128)] = (o1[...] + a1[0]) + (a1[1] + a1[2])
    tw2[:, lanes(at2, 128)] = o2[...] + a2[...]
    copies = []
    for peer in b_peers:
        here1 = tw1.at[own_rows, lanes(at1, 128)]
        here2 = tw2.at[:, lanes(at2, 128)]
        copies += [send(here1, here1, peer), send(here2, here2, peer)]
    far_bias = [send(o3, a3.at[k], a_peers[k]) for k in range(3)]
    wait(copies)
    piece1 = tw1.at[own_rows, lanes(y * 512, 512)]
    piece2 = tw2.at[:, lanes(core * 2048 + y * 512, 512)]
    back1 = {at: send(piece1, piece1, peer) for at, peer in xy_peers.items()}
    back2 = [send(piece2, piece2, peer) for peer in y_peers]
    wait(back2)
    here2 = tw2.at[:, lanes(core * 2048, 2048)]
    last2 = send(here2, here2, core_peer)
    store(here2, to_w2.at[:, lanes(core * 2048, 2048)])
    last = []
    for i in range(4):
        for j in range(4):
            if i or j:
                back1[i, j].wait()
        block = rows(8, core * 4 + flip(x, i))
        last.append(send(tw1.at[block, :], tw1.at[block, :], core_peer))
        store(tw1.at[block, :], to_w1.at[block, :])
    wait(far_bias)
    near = o3[...] + a3[0]
    tbias[...] = jnp.where(shared, near + (a3[1] + a3[2]), near)
    store(tbias, to_bias)
    wait(edges)
    tvol[:, 0, :] = inner[0] + jnp.where(me > 0, edge_in[0], 0.0)
    tvol[:, 3, :] = inner[1] + jnp.where(me < 7, edge_in[1], 0.0)
    store(tvol, to_vol)
    last2.wait()
    there = lanes((1 - core) * 2048, 2048)
    store(tw2.at[:, there], to_w2.at[:, there])
    for i in range(4):
        last[i].wait()
        block = rows(8, (1 - core) * 4 + flip(x, i))
        store(tw1.at[block, :], to_w1.at[block, :])
    wait(stored)


def stepped(vol, cot, w1, b1, w2, b2):
    shape = jax.ShapeDtypeStruct

    def vmem(*size):
        return pltpu.VMEM(size, F32)

    def half(*size):
        return pltpu.VMEM(size, BF16)

    return pl.pallas_call(
        step_kernel,
        out_shape=(
            shape((OWN, 128), F32),
            shape((MID, CIN * 64), F32),
            shape((OWN, MID * 64), F32),
            shape((8, 128), F32),
            shape((CIN, 4, 256), F32),
        ),
        in_specs=[
            pl.BlockSpec(memory_space=pltpu.HBM),
            pl.BlockSpec(memory_space=pltpu.HBM),
            pl.BlockSpec(memory_space=pltpu.HBM),
            pl.BlockSpec(memory_space=pltpu.HBM),
            pl.BlockSpec(memory_space=pltpu.HBM),
            pl.BlockSpec(memory_space=pltpu.HBM),
        ],
        out_specs=[pl.BlockSpec(memory_space=pltpu.HBM)] * 5,
        scratch_shapes=[
            vmem(OWN, 128), vmem(MID, CIN * 64), vmem(OWN, MID * 64), vmem(8, 128), vmem(CIN, 4, 256),
            vmem(CIN, 4, 256), vmem(4, CIN, 256), vmem(2, CIN, 256),
            vmem(8, MID + OWN, 128), vmem(MID, 128), vmem(8, OWN, 128), vmem(8, OWN, 128),
            vmem(MID, CIN * 64), vmem(2, 4, 8, OWN, 512), vmem(MID, 128), vmem(8, OWN, 128),
            vmem(1, MID), vmem(1, OWN),
            half(8, 512, 256), half(8, 512, 256), half(8, 256, 512), half(8, 128, 128),
            half(2, 4 * CIN, 512), half(4 * MID, 512), half(8 * CIN, 256), half(8, 2 * MID, 128),
            vmem(4 * CIN, 512),
            vmem(CIN * 64, 128), vmem(MID * 64, 128), half(CIN * 64, 256), half(MID * 64, 256),
            half(2 * MID, CIN * 64), half(2 * MID, MID * 64),
            vmem(MID, 128), vmem(32, CIN * 64), vmem(32, CIN * 64), vmem(OWN, MID * 64), vmem(8, 128),
            vmem(2, CIN, 256), vmem(2, CIN, 256), vmem(2, CIN, 256),
            vmem(32, 2048), vmem(8, 2048), vmem(8, 128),
            vmem(32, 2048), vmem(8, 2048), vmem(8, 128),
            vmem(15, 8, 512), vmem(3, 8, 128), vmem(8, 128),
            vmem(3, 8, 512), vmem(3, 8, 128),
            vmem(8, 512), vmem(8, 512), vmem(8, 128),
            vmem(3, 8, 128), vmem(3, 8, 128), vmem(3, 8, 128),
            vmem(8, 128), vmem(8, 128), vmem(8, 128),
            vmem(3, 8, 128), vmem(8, 128), vmem(3, 8, 128),
            pltpu.SemaphoreType.DMA((6,)),
            pltpu.SemaphoreType.DMA((16,)),
            pltpu.SemaphoreType.DMA((128,)),
            pltpu.SemaphoreType.DMA((128,)),
        ],
        compiler_params=pltpu.CompilerParams(
            collective_id=0, has_side_effects=True, vmem_limit_bytes=60 << 20
        ),
        name="stepped",
    )(vol, cot, w1, b1, w2, b2)


def finish_kernel(
    out, gw1, gw2, gbias, gvol, to_out, to_w1, to_w2, to_b1, to_b2, to_vol,
    out_here, w1_here, w2_here, bias_here, vol_here, done,
):
    through = [
        (gbias, bias_here, None),
        (gw1, w1_here, to_w1),
        (gw2, w2_here, to_w2),
        (gvol, vol_here, to_vol),
        (out, out_here, to_out),
    ]
    taken = [
        pltpu.make_async_copy(source, here, done.at[at])
        for at, (source, here, _) in enumerate(through)
    ]
    for copy in taken:
        copy.start()
    given = []
    for at, (_, here, target) in enumerate(through):
        taken[at].wait()
        if target is None:
            to_b1[...] = here[0, :MID]
            to_b2[...] = here[0, MID : MID + OWN]
        else:
            given.append(pltpu.make_async_copy(here, target, done.at[5 + at]))
            given[-1].start()
    for copy in given:
        copy.wait()


def finished(out, gw1, gw2, gbias, gvol):
    shape = jax.ShapeDtypeStruct
    anywhere = pl.BlockSpec(memory_space=pltpu.HBM)
    vmem = pl.BlockSpec(memory_space=pltpu.VMEM)
    return pl.pallas_call(
        finish_kernel,
        out_shape=(
            shape((OWN, 128), F32),
            shape((MID, CIN * 64), F32),
            shape((OWN, MID * 64), F32),
            shape((MID,), F32),
            shape((OWN,), F32),
            shape((CIN, 4, 256), F32),
        ),
        in_specs=[anywhere] * 5,
        out_specs=[anywhere, anywhere, anywhere, vmem, vmem, anywhere],
        scratch_shapes=[
            pltpu.VMEM((OWN, 128), F32),
            pltpu.VMEM((MID, CIN * 64), F32),
            pltpu.VMEM((OWN, MID * 64), F32),
            pltpu.VMEM((8, 128), F32),
            pltpu.VMEM((CIN, 4, 256), F32),
            pltpu.SemaphoreType.DMA((10,)),
        ],
        compiler_params=pltpu.CompilerParams(vmem_limit_bytes=60 << 20),
        name="finished",
    )(out, gw1, gw2, gbias, gvol)


def on_device(volume, cotangent, w_first, b_first, w_second, b_second):
    results = stepped(
        volume[0], cotangent[0], w_first, b_first[None], w_second, b_second[None]
    )
    out, gw1, gw2, gb1, gb2, gvol = finished(*results)
    return (out[None], gvol[None], gw1, gb1, gw2, gb2)


def solution(mesh):
    in_specs = (
        P("dp", None, "space", None),
        P("dp", "space", None),
        P(),
        P(),
        P("space", None),
        P("space"),
    )
    out_specs = (
        P("dp", "space", None),
        P("dp", None, "space", None),
        P(),
        P(),
        P("space", None),
        P("space"),
    )
    return jax.shard_map(
        on_device, mesh=mesh, in_specs=in_specs, out_specs=out_specs, check_vma=False
    )
```
